32 devices in a mesh: ctx: 16 (over z, y, x), tp: 2 (over core).
Axes of the slice: x: 2, y: 2, z: 4, core: 2. Of those that a mesh axis runs over, the one named last changes fastest.
Arguments:
- queries: bfloat16 [3072, 32, 128], P('ctx', 'tp'), may hold values from -6 to 6
- key_vectors: bfloat16 [3072, 4, 128], P('ctx', 'tp'), may hold values from -6 to 6
- value_matrix: bfloat16 [3072, 4, 128], P('ctx', 'tp'), may hold values from -6 to 6
- grad_out: bfloat16 [3072, 32, 128], P('ctx', 'tp'), may hold values from -6 to 6
- doc_lengths: int32 [8], replicated, may hold values from 1 to 1345, 3072 in all
Outputs:
- grad_queries: bfloat16 [3072, 32, 128], P('ctx', 'tp')
- grad_keys: bfloat16 [3072, 4, 128], P('ctx', 'tp')
- grad_values: bfloat16 [3072, 4, 128], P('ctx', 'tp')
The draws below stay inside these ranges and needn't reach their ends.
Inputs may be any that keep to these rules, and one draw needn't show every extreme that they name: `doc_lengths`: 8 document lengths that sum to 3072; the longest is exactly 1345.
All inputs are finite; a program needn't handle non-finite values.
Results may differ from the reference program's by a relative error of at most 0.0079.
Values may be sent and summed in bfloat16 or wider, within the bound.
No kernel may reach another device: no remote copies, remote signals or barrier semaphores. Data moves between devices by JAX's collectives and lax.ppermute only.
A program may use at most 64 MiB of HBM per device.

```python
import math
import jax
import jax.numpy as jnp
import numpy as np
from jax import lax

QUERY_HEADS = 32
VALUE_HEADS = 4
HEAD_SIZE = 128
TOK_DEV = 192
WIN = 8
SEQUENCE_TOKENS = 3072
MAXDOC = 1345
NDOCS = 8
N_CTX = 16


def draw_queries(key, part):
    array_shape = (SEQUENCE_TOKENS, QUERY_HEADS, HEAD_SIZE)
    noise = jnp.clip(jax.random.normal(jax.random.fold_in(key, 11), array_shape, jnp.float32), -4.0, 4.0)
    return noise.astype(jnp.bfloat16)


def draw_key_vectors(key, part):
    array_shape = (SEQUENCE_TOKENS, VALUE_HEADS, HEAD_SIZE)
    noise = jnp.clip(jax.random.normal(jax.random.fold_in(key, 12), array_shape, jnp.float32), -4.0, 4.0)
    return noise.astype(jnp.bfloat16)


def level_of(stream_key, shape, pieces, least, high):
    factor_of = 1.0
    for axis_at, parts in pieces:
        draws = jax.random.uniform(jax.random.fold_in(jax.random.fold_in(stream_key, 6), axis_at), (parts,), jnp.float32, least / len(pieces), high / len(pieces))
        factor_of = factor_of * jnp.repeat(jnp.exp(draws), shape[axis_at] // parts).reshape((-1,) + (1,) * (len(shape) - 1 - axis_at))
    return factor_of


def length_profile(count, total, limit, slope):
    weights = [(1 << 20) // math.isqrt(grade ** slope) + 1 for grade in range(2, count + 1)]
    surplus, counts = total - limit - (count - 1), [1] * (count - 1)
    while surplus > 0:
        free = [i for i in range(count - 1) if counts[i] < limit]
        whole, left = sum([weights[i] for i in free]), surplus
        for i in free:
            addition = min(limit - counts[i], max(1, left * weights[i] // whole), surplus)
            counts[i] = counts[i] + addition
            surplus = surplus - addition
    return np.array([limit] + counts)


def ragged_sizes(key, number_of, total, most, skew):
    if number_of == 2:
        one = jax.random.randint(key, (), max(1, total - most), min(most, total - 1) + 1)
        return jnp.stack([one, total - one])
    tallies = jnp.asarray(length_profile(number_of, total, most, skew), jnp.int32)
    pairs = (number_of - 1) // 2
    source_of, receiver = tallies[1:1 + 2 * pairs:2], tallies[2:2 + 2 * pairs:2]
    slack = jnp.minimum(source_of - 1, most - receiver)
    moved = jax.random.randint(jax.random.fold_in(key, 1), (pairs,), 0, 1 << 20) % (slack + 1)
    tallies = tallies.at[1:1 + 2 * pairs:2].set(source_of - moved).at[2:2 + 2 * pairs:2].set(receiver + moved)
    return tallies[jax.random.permutation(jax.random.fold_in(key, 2), number_of)]


def gaussian(key, dims, width, limit, split=(), held_as=jnp.bfloat16):
    drawn = jax.random.normal(key, dims, jnp.float32) * width
    if len(split) > 0:
        drawn = level_of(key, dims, split, -0.22, 0.18) * drawn
    return jnp.clip(drawn, min=-limit, max=limit).astype(held_as)


def setup_inputs(seed: int = 0) -> dict:
    arg_keys = jax.random.split(jax.random.key(seed), 6)
    return {
        "queries": draw_queries(jax.random.fold_in(arg_keys[5], 71), 0),
        "key_vectors": draw_key_vectors(jax.random.fold_in(arg_keys[5], 71), 0),
        "value_matrix": gaussian(arg_keys[2], (SEQUENCE_TOKENS, VALUE_HEADS, HEAD_SIZE), 1.0, 6.0, ((0, 16), (1, 2))),
        "grad_out": gaussian(arg_keys[3], (SEQUENCE_TOKENS, QUERY_HEADS, HEAD_SIZE), 1.0, 6.0, ((0, 16), (1, 2))),
        "doc_lengths": ragged_sizes(arg_keys[4], NDOCS, SEQUENCE_TOKENS, MAXDOC, 2).astype(jnp.int32),
    }


neg_fill = -1.0e30


def doc_index(positions, lengths):
    doc_ends = jnp.cumsum(lengths)
    return jnp.sum((positions[:, None] >= doc_ends[None, :]).astype(jnp.int32), axis=1).astype(jnp.int32)


def reference(queries, key_vectors, value_matrix, grad_out, doc_lengths):
    stripe = TOK_DEV
    key_span = WIN * TOK_DEV
    leading_rows = key_span - stripe
    head_groups = VALUE_HEADS
    repeat_factor = QUERY_HEADS // VALUE_HEADS
    softmax_scale = HEAD_SIZE ** -0.5
    highest = lax.Precision.HIGHEST
    leading_zeros = jnp.zeros((leading_rows, VALUE_HEADS, HEAD_SIZE), jnp.float32)
    padded_keys = jnp.concatenate([leading_zeros, key_vectors.astype(jnp.float32)], axis=0)
    padded_values = jnp.concatenate([leading_zeros, value_matrix.astype(jnp.float32)], axis=0)
    query_all = queries.astype(jnp.float32).reshape(N_CTX, stripe, head_groups, repeat_factor, HEAD_SIZE)
    grad_all = grad_out.astype(jnp.float32).reshape(N_CTX, stripe, head_groups, repeat_factor, HEAD_SIZE)
    numbers = jnp.arange(N_CTX, dtype=jnp.int32)

    def one_stripe(carried, inputs):
        key_acc, value_acc = carried
        query_rows, grad_rows, number = inputs
        start = (number * stripe).astype(jnp.int32)
        key_win = lax.dynamic_slice_in_dim(padded_keys, start, key_span, 0)
        value_win = lax.dynamic_slice_in_dim(padded_values, start, key_span, 0)
        query_pos = start + jnp.arange(stripe, dtype=jnp.int32)
        key_pos = start - leading_rows + jnp.arange(key_span, dtype=jnp.int32)
        same_doc = doc_index(key_pos, doc_lengths)[None, :] == doc_index(query_pos, doc_lengths)[:, None]
        live_pairs = (key_pos[None, :] <= query_pos[:, None]) & (key_pos[None, :] >= 0) & same_doc
        raw_scores = jnp.einsum("qgrd,kgd->grqk", query_rows, key_win, precision=highest) * softmax_scale
        logits = jnp.where(live_pairs, raw_scores, neg_fill)
        row_max = jnp.max(logits, axis=-1, keepdims=True)
        row_sum = jnp.sum(jnp.where(live_pairs, jnp.exp(logits - row_max), 0.0), axis=-1, keepdims=True)
        log_total = row_max + jnp.log(row_sum)
        probs = jnp.where(live_pairs, jnp.exp(logits - log_total), 0.0)
        grad_probs = jnp.einsum("qgrd,kgd->grqk", grad_rows, value_win, precision=highest)
        row_dots = jnp.sum(probs * grad_probs, axis=-1, keepdims=True)
        grad_scores = lax.optimization_barrier((probs * (grad_probs - row_dots)).astype(jnp.bfloat16)).astype(jnp.float32)
        probs_low = lax.optimization_barrier(probs.astype(jnp.bfloat16)).astype(jnp.float32)
        query_grad = jnp.einsum("grqk,kgd->qgrd", grad_scores, key_win, precision=highest) * softmax_scale
        key_grad = jnp.einsum("grqk,qgrd->kgd", grad_scores, query_rows, precision=highest) * softmax_scale
        value_grad = jnp.einsum("grqk,qgrd->kgd", probs_low, grad_rows, precision=highest)
        key_acc = lax.dynamic_update_slice_in_dim(key_acc, lax.dynamic_slice_in_dim(key_acc, start, key_span, 0) + key_grad, start, 0)
        value_acc = lax.dynamic_update_slice_in_dim(value_acc, lax.dynamic_slice_in_dim(value_acc, start, key_span, 0) + value_grad, start, 0)
        return (key_acc, value_acc), query_grad.reshape(stripe, QUERY_HEADS, HEAD_SIZE).astype(jnp.bfloat16)

    initial_accumulator = jnp.zeros((leading_rows + SEQUENCE_TOKENS, VALUE_HEADS, HEAD_SIZE), jnp.float32)
    (key_acc, value_acc), query_parts = lax.scan(one_stripe, (initial_accumulator, initial_accumulator), (query_all, grad_all, numbers))
    grad_queries = query_parts.reshape(SEQUENCE_TOKENS, QUERY_HEADS, HEAD_SIZE)
    grad_keys = key_acc[leading_rows:].astype(jnp.bfloat16)
    grad_values = value_acc[leading_rows:].astype(jnp.bfloat16)
    return (grad_queries, grad_keys, grad_values)
```

```python
import functools
import math

import jax
import jax.numpy as jnp
from jax import lax
from jax.experimental import pallas as pl
from jax.experimental.pallas import tpu as pltpu
from jax.sharding import PartitionSpec as P

MAXDOC = 1345
PLANE = 4
FLIPS = (1, 2, 3)
LOG2E = math.log2(math.e)
NEG_INIT = -1e30
NEG_DEAD = -2e30
CHUNK = 512

NT = (((1,), (1,)), ((), ()))
NN = (((1,), (0,)), ((), ()))
TN = (((0,), (0,)), ((), ()))


def mm(a, b, dims):
    return lax.dot_general(a, b, dims, preferred_element_type=jnp.float32)


def kernel(heads_per, n_docs, *refs):
    (place_ref, lens_ref, q_ref, do_ref, own_ref, up_ref) = refs[:6]
    near_refs, far_refs, upx_refs = refs[6:9], refs[9:12], refs[12:15]
    dq_ref = refs[15]
    part_refs = refs[16:24]
    kv, part, m_ref, l_ref, d_ref, dqt, start_ref, pos_ref, stripe_ref = refs[24:]
    groups, cols, dim = q_ref.shape
    stripe = own_ref.shape[2]
    scale = dim**-0.5
    scale2 = scale * LOG2E
    me = place_ref[0]
    lane = lax.rem(me, PLANE)
    first_pos = me * stripe

    col = lax.broadcasted_iota(jnp.int32, (1, cols), 1)
    pos = first_pos + lax.div(col, heads_per)
    start = jnp.zeros((1, cols), jnp.int32)
    end = jnp.int32(0)
    first_key = jnp.int32(0)
    for n in range(n_docs):
        end = end + lens_ref[n]
        start = jnp.maximum(start, jnp.where(pos >= end, end, 0))
        first_key = jnp.maximum(first_key, jnp.where(first_pos >= end, end, 0))
    start_ref[...] = start
    pos_ref[...] = pos

    kv[0] = own_ref[...]
    kv[1] = up_ref[...]
    stripe_ref[0] = me
    stripe_ref[1] = me - PLANE
    for k, flip in enumerate(FLIPS):
        other = jnp.bitwise_xor(lane, flip)
        is_near = other < lane
        kv[2 + k] = upx_refs[k][...]
        stripe_ref[2 + k] = me - PLANE - lane + other

        @pl.when(is_near)
        def _():
            kv[5 + k] = near_refs[k][...]

        @pl.when(jnp.logical_not(is_near))
        def _():
            kv[5 + k] = far_refs[k][...]

        stripe_ref[5 + k] = jnp.where(is_near, me - lane + other, me - 2 * PLANE - lane + other)

    m_ref[...] = jnp.full_like(m_ref, NEG_INIT)
    l_ref[...] = jnp.zeros_like(l_ref)
    d_ref[...] = jnp.zeros_like(d_ref)
    dqt[...] = jnp.zeros_like(dqt)

    def logits(keys, q_c, base, cs):
        s = mm(keys, q_c, NT) * scale2
        kpos = base + lax.broadcasted_iota(jnp.int32, s.shape, 0)
        live = (kpos >= start_ref[:, cs]) & (kpos <= pos_ref[:, cs])
        return jnp.where(live, s, NEG_DEAD)

    def is_live(slot):
        at = stripe_ref[slot]
        return (at >= 0) & ((at + 1) * stripe > first_key)

    def stats_step(i, carry):
        slot, g = lax.div(i, groups), lax.rem(i, groups)

        @pl.when(is_live(slot))
        def _():
            base = stripe_ref[slot] * stripe
            keys, vals = kv[slot, 0, g], kv[slot, 1, g]
            for c in range(0, cols, CHUNK):
                cs = pl.ds(c, CHUNK)
                s = logits(keys, q_ref[g, cs, :], base, cs)
                gp = mm(vals, do_ref[g, cs, :], NT)
                m_old = m_ref[g, :, cs]
                m_new = jnp.maximum(m_old, jnp.max(s, axis=0, keepdims=True))
                e = jnp.exp2(s - m_new)
                fade = jnp.exp2(m_old - m_new)
                m_ref[g, :, cs] = m_new
                l_ref[g, :, cs] = l_ref[g, :, cs] * fade + jnp.sum(e, axis=0, keepdims=True)
                d_ref[g, :, cs] = d_ref[g, :, cs] * fade + jnp.sum(e * gp, axis=0, keepdims=True)

        return carry

    lax.fori_loop(0, 8 * groups, stats_step, 0)
    d_ref[...] = d_ref[...] / l_ref[...]
    m_ref[...] = m_ref[...] + jnp.log2(l_ref[...])

    def grad_step(i, carry):
        slot, g = lax.div(i, groups), lax.rem(i, groups)
        live = is_live(slot)

        @pl.when(live)
        def _():
            base = stripe_ref[slot] * stripe
            keys, vals = kv[slot, 0, g], kv[slot, 1, g]
            dk = jnp.zeros((stripe, dim), jnp.float32)
            dv = jnp.zeros((stripe, dim), jnp.float32)
            for c in range(0, cols, CHUNK):
                cs = pl.ds(c, CHUNK)
                q_c, do_c = q_ref[g, cs, :], do_ref[g, cs, :]
                s = logits(keys, q_c, base, cs)
                gp = mm(vals, do_c, NT)
                p = jnp.exp2(s - m_ref[g, :, cs])
                ds = (p * (gp - d_ref[g, :, cs])).astype(jnp.bfloat16)
                dv = dv + mm(p.astype(jnp.bfloat16), do_c, NN)
                dk = dk + mm(ds, q_c, NN)
                dqt[g, :, cs] = dqt[g, :, cs] + mm(keys, ds, TN)
            part[slot, 0, g] = (dk * scale).astype(jnp.bfloat16)
            part[slot, 1, g] = dv.astype(jnp.bfloat16)

        @pl.when(jnp.logical_not(live))
        def _():
            part[slot, 0, g] = jnp.zeros((stripe, dim), jnp.bfloat16)
            part[slot, 1, g] = jnp.zeros((stripe, dim), jnp.bfloat16)

        return carry

    lax.fori_loop(0, 8 * groups, grad_step, 0)
    for n in range(8):
        part_refs[n][...] = part[n]
    for g in range(groups):
        dq_ref[g] = (dqt[g] * scale).T.astype(jnp.bfloat16)


def shards(queries, key_vectors, value_matrix, grad_out, doc_lengths):
    stripe, heads, dim = queries.shape
    groups = key_vectors.shape[1]
    heads_per = heads // groups
    cols = stripe * heads_per
    length = lax.axis_size("ctx")
    me = lax.axis_index("ctx").astype(jnp.int32)
    lane = lax.rem(me, PLANE)

    def send(array, to):
        pairs = [(i, to(i)) for i in range(length) if to(i) is not None and 0 <= to(i) < length]
        return lax.ppermute(array, "ctx", pairs)

    def flip_if(flip, test):
        return lambda i: (i ^ flip) if test(i ^ flip, i) else None

    own = jnp.stack([key_vectors, value_matrix]).transpose(0, 2, 1, 3)
    up = send(own, lambda i: i + PLANE)
    near = [send(own, flip_if(f, lambda to, i: to > i)) for f in FLIPS]
    upx = [send(up, lambda i, f=f: i ^ f) for f in FLIPS]
    up2 = send(up, lambda i: i + PLANE)
    far = [send(up2, flip_if(f, lambda to, i: to < i)) for f in FLIPS]

    def columns(array):
        return array.reshape(stripe, groups, heads_per, dim).transpose(1, 0, 2, 3).reshape(groups, cols, dim)

    q, do = columns(queries), columns(grad_out)
    smem = pl.BlockSpec(memory_space=pltpu.SMEM)
    vmem = pl.BlockSpec(memory_space=pltpu.VMEM)
    piece = jax.ShapeDtypeStruct(own.shape, jnp.bfloat16)
    stat = pltpu.VMEM((groups, 1, cols), jnp.float32)
    row = pltpu.VMEM((1, cols), jnp.int32)
    outs = pl.pallas_call(
        functools.partial(kernel, heads_per, doc_lengths.shape[0]),
        out_shape=[jax.ShapeDtypeStruct(q.shape, jnp.bfloat16)] + [piece] * 8,
        in_specs=[smem, smem] + [vmem] * 13,
        out_specs=[vmem] * 9,
        scratch_shapes=[
            pltpu.VMEM((8,) + own.shape, jnp.bfloat16),
            pltpu.VMEM((8,) + own.shape, jnp.bfloat16),
            stat,
            stat,
            stat,
            pltpu.VMEM((groups, dim, cols), jnp.float32),
            row,
            row,
            pltpu.SMEM((8,), jnp.int32),
        ],
        compiler_params=pltpu.CompilerParams(vmem_limit_bytes=40 << 20),
    )(me[None], doc_lengths, q, do, own, up, *near, *far, *upx)
    dq, parts = outs[0], outs[1:]
    mixed = [send(parts[5 + k], lambda i, f=f: i ^ f).astype(jnp.float32) for k, f in enumerate(FLIPS)]
    level = [send(parts[2 + k], lambda i, f=f: i ^ f).astype(jnp.float32) for k, f in enumerate(FLIPS)]
    mine = parts[0].astype(jnp.float32)
    far_sum = jnp.zeros_like(mine)
    for k, flip in enumerate(FLIPS):
        other = jnp.bitwise_xor(lane, flip)
        mine = mine + jnp.where(other > lane, mixed[k], 0.0)
        far_sum = far_sum + jnp.where(other < lane, mixed[k], 0.0)
    down2 = send(far_sum.astype(jnp.bfloat16), lambda i: i - PLANE).astype(jnp.float32)
    level_sum = parts[1].astype(jnp.float32) + sum(level) + down2
    down = send(level_sum.astype(jnp.bfloat16), lambda i: i - PLANE).astype(jnp.float32)
    total = (mine + down).astype(jnp.bfloat16).transpose(0, 2, 1, 3)
    dq = dq.reshape(groups, stripe, heads_per, dim).transpose(1, 0, 2, 3).reshape(stripe, heads, dim)
    return dq, total[0], total[1]


def solution(mesh):
    spec = P("ctx", "tp", None)
    return jax.shard_map(
        shards,
        mesh=mesh,
        in_specs=(spec, spec, spec, spec, P()),
        out_specs=(spec, spec, spec),
        check_vma=False,
    )
```

```python
import functools
import math

import jax
import jax.numpy as jnp
from jax import lax
from jax.experimental import pallas as pl
from jax.experimental.pallas import tpu as pltpu
from jax.sharding import PartitionSpec as P

PLANE = 4
FLIPS = (1, 2, 3)
LOG2E = math.log2(math.e)
NEG_INIT = -1e30
NEG_DEAD = -2e30
CHUNK = 512

NT = (((1,), (1,)), ((), ()))
NN = (((1,), (0,)), ((), ()))
TN = (((0,), (0,)), ((), ()))
SMEM = pl.BlockSpec(memory_space=pltpu.SMEM)
VMEM = pl.BlockSpec(memory_space=pltpu.VMEM)


def mm(a, b, dims):
    return lax.dot_general(a, b, dims, preferred_element_type=jnp.float32)


def own_slot(me, lane):
    return me


def up_slot(me, lane):
    return me - PLANE


def upx_slot(flip, me, lane):
    return me - PLANE - lane + jnp.bitwise_xor(lane, flip)


def mix_slot(flip, me, lane):
    other = jnp.bitwise_xor(lane, flip)
    return me - lane + other - jnp.where(other < lane, 0, 2 * PLANE)


def mark_rows(place_ref, lens_ref, n_docs, stripe, heads_per, start_ref, pos_ref):
    me = place_ref[0]
    first_pos = me * stripe
    col = lax.broadcasted_iota(jnp.int32, start_ref.shape, 1)
    pos = first_pos + lax.div(col, heads_per)
    start = jnp.zeros(start_ref.shape, jnp.int32)
    end = jnp.int32(0)
    first_key = jnp.int32(0)
    for n in range(n_docs):
        end = end + lens_ref[n]
        start = jnp.maximum(start, jnp.where(pos >= end, end, 0))
        first_key = jnp.maximum(first_key, jnp.where(first_pos >= end, end, 0))
    start_ref[...] = start
    pos_ref[...] = pos
    return me, lax.rem(me, PLANE), first_key


def logits(keys, q_c, base, cs, start_ref, pos_ref, scale2):
    s = mm(keys, q_c, NT) * scale2
    kpos = base + lax.broadcasted_iota(jnp.int32, s.shape, 0)
    live = (kpos >= start_ref[:, cs]) & (kpos <= pos_ref[:, cs])
    return jnp.where(live, s, NEG_DEAD)


def stats_kernel(slots, heads_per, n_docs, first, last, *refs):
    n = len(slots)
    place_ref, lens_ref, q_ref, do_ref = refs[:4]
    kv_refs = refs[4 : 4 + n]
    refs = refs[4 + n :]
    if not first:
        m_in, l_in, d_in = refs[:3]
        refs = refs[3:]
    m_ref, l_ref, d_ref, start_ref, pos_ref = refs
    groups, cols, dim = q_ref.shape
    stripe = kv_refs[0].shape[2]
    scale2 = dim**-0.5 * LOG2E
    me, lane, first_key = mark_rows(place_ref, lens_ref, n_docs, stripe, heads_per, start_ref, pos_ref)
    if first:
        m_ref[...] = jnp.full_like(m_ref, NEG_INIT)
        l_ref[...] = jnp.zeros_like(l_ref)
        d_ref[...] = jnp.zeros_like(d_ref)
    else:
        m_ref[...] = m_in[...]
        l_ref[...] = l_in[...]
        d_ref[...] = d_in[...]
    for kv_ref, slot in zip(kv_refs, slots):
        at = slot(me, lane)

        @pl.when((at >= 0) & ((at + 1) * stripe > first_key))
        def _():
            base = at * stripe

            @pl.loop(0, groups)
            def _(g):
                keys, vals = kv_ref[0, g], kv_ref[1, g]
                for c in range(0, cols, CHUNK):
                    cs = pl.ds(c, CHUNK)
                    s = logits(keys, q_ref[g, cs, :], base, cs, start_ref, pos_ref, scale2)
                    gp = mm(vals, do_ref[g, cs, :], NT)
                    m_old = m_ref[g, :, cs]
                    m_new = jnp.maximum(m_old, jnp.max(s, axis=0, keepdims=True))
                    e = jnp.exp2(s - m_new)
                    fade = jnp.exp2(m_old - m_new)
                    m_ref[g, :, cs] = m_new
                    l_ref[g, :, cs] = l_ref[g, :, cs] * fade + jnp.sum(e, axis=0, keepdims=True)
                    d_ref[g, :, cs] = d_ref[g, :, cs] * fade + jnp.sum(e * gp, axis=0, keepdims=True)

    if last:
        d_ref[...] = d_ref[...] / l_ref[...]
        m_ref[...] = m_ref[...] + jnp.log2(l_ref[...])


def grad_kernel(slots, heads_per, n_docs, first, last, *refs):
    n = len(slots)
    place_ref, lens_ref, q_ref, do_ref, m_ref, d_ref = refs[:6]
    kv_refs = refs[6 : 6 + n]
    refs = refs[6 + n :]
    if not first:
        dq_in = refs[0]
        refs = refs[1:]
    part_refs = refs[:n]
    dq_out = refs[n]
    start_ref, pos_ref = refs[n + 1 : n + 3]
    groups, cols, dim = q_ref.shape
    stripe = kv_refs[0].shape[2]
    scale = dim**-0.5
    scale2 = scale * LOG2E
    me, lane, first_key = mark_rows(place_ref, lens_ref, n_docs, stripe, heads_per, start_ref, pos_ref)
    dqt = refs[n + 3] if last else dq_out
    if first:
        dqt[...] = jnp.zeros_like(dqt)
    else:
        dqt[...] = dq_in[...]
    for kv_ref, part_ref, slot in zip(kv_refs, part_refs, slots):
        at = slot(me, lane)
        live = (at >= 0) & ((at + 1) * stripe > first_key)

        @pl.when(live)
        def _():
            base = at * stripe

            @pl.loop(0, groups)
            def _(g):
                keys, vals = kv_ref[0, g], kv_ref[1, g]
                dk = jnp.zeros((stripe, dim), jnp.float32)
                dv = jnp.zeros((stripe, dim), jnp.float32)
                for c in range(0, cols, CHUNK):
                    cs = pl.ds(c, CHUNK)
                    q_c, do_c = q_ref[g, cs, :], do_ref[g, cs, :]
                    s = logits(keys, q_c, base, cs, start_ref, pos_ref, scale2)
                    gp = mm(vals, do_c, NT)
                    p = jnp.exp2(s - m_ref[g, :, cs])
                    ds = (p * (gp - d_ref[g, :, cs])).astype(jnp.bfloat16)
                    dv = dv + mm(p.astype(jnp.bfloat16), do_c, NN)
                    dk = dk + mm(ds, q_c, NN)
                    dqt[g, :, cs] = dqt[g, :, cs] + mm(keys, ds, TN)
                part_ref[0, g] = (dk * scale).astype(jnp.bfloat16)
                part_ref[1, g] = dv.astype(jnp.bfloat16)

        @pl.when(jnp.logical_not(live))
        def _():
            part_ref[...] = jnp.zeros_like(part_ref)

    if last:
        for g in range(groups):
            dq_out[g] = (dqt[g] * scale).T.astype(jnp.bfloat16)


def shards(queries, key_vectors, value_matrix, grad_out, doc_lengths):
    stripe, heads, dim = queries.shape
    groups = key_vectors.shape[1]
    heads_per = heads // groups
    cols = stripe * heads_per
    length = lax.axis_size("ctx")
    me = lax.axis_index("ctx").astype(jnp.int32)
    lane = lax.rem(me, PLANE)
    place = me[None]

    def send(array, to):
        pairs = [(i, to(i)) for i in range(length) if 0 <= to(i) < length]
        return lax.ppermute(array, "ctx", pairs)

    def columns(array):
        return array.reshape(stripe, groups, heads_per, dim).transpose(1, 0, 2, 3).reshape(groups, cols, dim)

    own = jnp.stack([key_vectors, value_matrix]).transpose(0, 2, 1, 3)
    q, do = columns(queries), columns(grad_out)
    piece = jax.ShapeDtypeStruct(own.shape, jnp.bfloat16)
    stat = jax.ShapeDtypeStruct((groups, 1, cols), jnp.float32)
    total = jax.ShapeDtypeStruct((groups, dim, cols), jnp.float32)
    row = pltpu.VMEM((1, cols), jnp.int32)
    n_docs = doc_lengths.shape[0]
    pair_flops = groups * stripe * cols * dim * 2

    def params(products, n):
        return dict(
            compiler_params=pltpu.CompilerParams(vmem_limit_bytes=20 << 20),
            cost_estimate=pl.CostEstimate(flops=products * n * pair_flops * 2, bytes_accessed=1 << 20, transcendentals=0),
        )

    def stats(slots, kvs, old=None, last=False):
        return pl.pallas_call(
            functools.partial(stats_kernel, slots, heads_per, n_docs, old is None, last),
            out_shape=[stat] * 3,
            in_specs=[SMEM, SMEM] + [VMEM] * (2 + len(kvs) + (0 if old is None else 3)),
            out_specs=[VMEM] * 3,
            scratch_shapes=[row, row],
            **params(2, len(kvs)),
        )(place, doc_lengths, q, do, *kvs, *(old or ()))

    def grads(slots, kvs, m, d, old=None, last=False):
        n = len(kvs)
        dq_shape = jax.ShapeDtypeStruct(q.shape, jnp.bfloat16) if last else total
        outs = pl.pallas_call(
            functools.partial(grad_kernel, slots, heads_per, n_docs, old is None, last),
            out_shape=[piece] * n + [dq_shape],
            in_specs=[SMEM, SMEM] + [VMEM] * (4 + n + (0 if old is None else 1)),
            out_specs=[VMEM] * (n + 1),
            scratch_shapes=[row, row] + ([pltpu.VMEM(total.shape, jnp.float32)] if last else []),
            **params(5, n),
        )(place, doc_lengths, q, do, m, d, *kvs, *(() if old is None else (old,)))
        return outs[:n], outs[n]

    upx_slots = [functools.partial(upx_slot, f) for f in FLIPS]
    mix_slots = [functools.partial(mix_slot, f) for f in FLIPS]
    other = [jnp.bitwise_xor(lane, f) for f in FLIPS]

    up = send(own, lambda i: i + PLANE)
    seen = stats([own_slot], [own])
    up, seen = lax.optimization_barrier((up, seen))
    up2 = send(up, lambda i: i + PLANE)
    upx = [send(up, lambda i, f=f: i ^ f) for f in FLIPS]
    seen = stats([up_slot], [up], seen)
    mix = [send(jnp.where(other[k] > lane, own, up2), lambda i, f=f: i ^ f) for k, f in enumerate(FLIPS)]
    seen = stats(upx_slots, upx, seen)
    m, _, d = stats(mix_slots, mix, seen, last=True)

    mix_parts, dq = grads(mix_slots, mix, m, d)
    mixed = [send(part, lambda i, f=f: i ^ f) for part, f in zip(mix_parts, FLIPS)]
    upx_parts, dq = grads(upx_slots, upx, m, d, dq)
    level = [send(part, lambda i, f=f: i ^ f) for part, f in zip(upx_parts, FLIPS)]
    (up_part, own_part), dq = grads([up_slot, own_slot], [up, own], m, d, dq, last=True)

    wide = [x.astype(jnp.float32) for x in mixed]
    far_sum = sum(jnp.where(other[k] < lane, wide[k], 0.0) for k in range(3))
    down2 = send(far_sum.astype(jnp.bfloat16), lambda i: i - PLANE).astype(jnp.float32)
    level_sum = up_part.astype(jnp.float32) + sum(x.astype(jnp.float32) for x in level) + down2
    down = send(level_sum.astype(jnp.bfloat16), lambda i: i - PLANE).astype(jnp.float32)
    mine = own_part.astype(jnp.float32) + sum(jnp.where(other[k] > lane, wide[k], 0.0) for k in range(3))
    kv_grad = (mine + down).astype(jnp.bfloat16).transpose(0, 2, 1, 3)
    dq = dq.reshape(groups, stripe, heads_per, dim).transpose(1, 0, 2, 3).reshape(stripe, heads, dim)
    return dq, kv_grad[0], kv_grad[1]


def solution(mesh):
    spec = P("ctx", "tp", None)
    return jax.shard_map(
        shards,
        mesh=mesh,
        in_specs=(spec, spec, spec, spec, P()),
        out_specs=(spec, spec, spec),
        check_vma=False,
    )
```

```python
import functools
import math

import jax
import jax.numpy as jnp
from jax import lax
from jax.experimental import pallas as pl
from jax.experimental.pallas import tpu as pltpu
from jax.sharding import PartitionSpec as P


PLANE = 4
FLIPS = (1, 2, 3)
LOG2E = math.log2(math.e)
NEG_INIT = -1e30
NEG_DEAD = -2e30
CHUNK = 512

NT = (((1,), (1,)), ((), ()))
NN = (((1,), (0,)), ((), ()))
TN = (((0,), (0,)), ((), ()))
SMEM = pl.BlockSpec(memory_space=pltpu.SMEM)
VMEM = pl.BlockSpec(memory_space=pltpu.VMEM)


def mm(a, b, dims):
    return lax.dot_general(a, b, dims, preferred_element_type=jnp.float32)


def own_slot(me, lane):
    return me


def up_slot(me, lane):
    return me - PLANE


def upx_slot(flip, me, lane):
    return me - PLANE - lane + jnp.bitwise_xor(lane, flip)


def mix_slot(flip, me, lane):
    other = jnp.bitwise_xor(lane, flip)
    return me - lane + other - jnp.where(other < lane, 0, 2 * PLANE)


def pieces(refs, slots):
    for ref, held in zip(refs, slots):
        for k, slot in enumerate(held):
            yield ref.at[k], slot


def mark_rows(place_ref, lens_ref, n_docs, stripe, heads_per, start_ref, pos_ref):
    me = place_ref[0]
    first_pos = me * stripe
    col = lax.broadcasted_iota(jnp.int32, start_ref.shape, 1)
    pos = first_pos + lax.div(col, heads_per)
    start = jnp.zeros(start_ref.shape, jnp.int32)
    end = jnp.int32(0)
    first_key = jnp.int32(0)
    for n in range(n_docs):
        end = end + lens_ref[n]
        start = jnp.maximum(start, jnp.where(pos >= end, end, 0))
        first_key = jnp.maximum(first_key, jnp.where(first_pos >= end, end, 0))
    start_ref[...] = start
    pos_ref[...] = pos
    return me, lax.rem(me, PLANE), first_key


def logits(keys, q_c, base, cs, start_ref, pos_ref, scale2):
    s = mm(keys, q_c, NT) * scale2
    kpos = base + lax.broadcasted_iota(jnp.int32, s.shape, 0)
    live = (kpos >= start_ref[:, cs]) & (kpos <= pos_ref[:, cs])
    return jnp.where(live, s, NEG_DEAD)


def stats_kernel(slots, heads_per, n_docs, first, last, *refs):
    n = len(slots)
    place_ref, lens_ref, q_ref, do_ref = refs[:4]
    kv_refs = refs[4 : 4 + n]
    refs = refs[4 + n :]
    if not first:
        refs = refs[3:]
    m_ref, l_ref, d_ref, start_ref, pos_ref = refs
    groups, cols, dim = q_ref.shape
    stripe = kv_refs[0].shape[-2]
    scale2 = dim**-0.5 * LOG2E
    me, lane, first_key = mark_rows(place_ref, lens_ref, n_docs, stripe, heads_per, start_ref, pos_ref)
    if first:
        m_ref[...] = jnp.full_like(m_ref, NEG_INIT)
        l_ref[...] = jnp.zeros_like(l_ref)
        d_ref[...] = jnp.zeros_like(d_ref)
    for kv_ref, slot in pieces(kv_refs, slots):
        at = slot(me, lane)

        @pl.when((at >= 0) & ((at + 1) * stripe > first_key))
        def _():
            base = at * stripe

            @pl.loop(0, groups)
            def _(g):
                keys, vals = kv_ref[0, g], kv_ref[1, g]
                for c in range(0, cols, CHUNK):
                    cs = pl.ds(c, CHUNK)
                    s = logits(keys, q_ref[g, cs, :], base, cs, start_ref, pos_ref, scale2)
                    gp = mm(vals, do_ref[g, cs, :], NT)
                    m_old = m_ref[g, :, cs]
                    m_new = jnp.maximum(m_old, jnp.max(s, axis=0, keepdims=True))
                    e = jnp.exp2(s - m_new)
                    fade = jnp.exp2(m_old - m_new)
                    m_ref[g, :, cs] = m_new
                    l_ref[g, :, cs] = l_ref[g, :, cs] * fade + jnp.sum(e, axis=0, keepdims=True)
                    d_ref[g, :, cs] = d_ref[g, :, cs] * fade + jnp.sum(e * gp, axis=0, keepdims=True)

    if last:
        d_ref[...] = d_ref[...] / l_ref[...]
        m_ref[...] = m_ref[...] + jnp.log2(l_ref[...])


def grad_kernel(slots, heads_per, n_docs, first, last, *refs):
    n = len(slots)
    place_ref, lens_ref, q_ref, do_ref, m_ref, d_ref = refs[:6]
    kv_refs = refs[6 : 6 + n]
    refs = refs[6 + n :]
    if not first:
        refs = refs[1:]
    part_refs = refs[:n]
    dqt, start_ref, pos_ref = refs[n : n + 3] if not last else refs[n + 1 : n + 4]
    groups, cols, dim = q_ref.shape
    stripe = kv_refs[0].shape[-2]
    scale = dim**-0.5
    scale2 = scale * LOG2E
    me, lane, first_key = mark_rows(place_ref, lens_ref, n_docs, stripe, heads_per, start_ref, pos_ref)
    if first:
        dqt[...] = jnp.zeros_like(dqt)
    for (kv_ref, slot), (part_ref, _) in zip(pieces(kv_refs, slots), pieces(part_refs, slots)):
        at = slot(me, lane)
        live = (at >= 0) & ((at + 1) * stripe > first_key)

        @pl.when(live)
        def _():
            base = at * stripe

            @pl.loop(0, groups)
            def _(g):
                keys, vals = kv_ref[0, g], kv_ref[1, g]
                dk = jnp.zeros((stripe, dim), jnp.float32)
                dv = jnp.zeros((stripe, dim), jnp.float32)
                for c in range(0, cols, CHUNK):
                    cs = pl.ds(c, CHUNK)
                    q_c, do_c = q_ref[g, cs, :], do_ref[g, cs, :]
                    s = logits(keys, q_c, base, cs, start_ref, pos_ref, scale2)
                    gp = mm(vals, do_c, NT)
                    p = jnp.exp2(s - m_ref[g, :, cs])
                    ds = (p * (gp - d_ref[g, :, cs])).astype(jnp.bfloat16)
                    dv = dv + mm(p.astype(jnp.bfloat16), do_c, NN)
                    dk = dk + mm(ds, q_c, NN)
                    dqt[g, :, cs] = dqt[g, :, cs] + mm(keys, ds, TN)
                part_ref[0, g] = (dk * scale).astype(jnp.bfloat16)
                part_ref[1, g] = dv.astype(jnp.bfloat16)

        @pl.when(jnp.logical_not(live))
        def _():
            part_ref[...] = jnp.zeros_like(part_ref)

    if last:
        for g in range(groups):
            refs[n][g] = (dqt[g] * scale).T.astype(jnp.bfloat16)


def pack_kernel(k_ref, v_ref, own_ref, wide):
    groups, stripe = own_ref.shape[-3:-1]
    for n, ref in enumerate((k_ref, v_ref)):
        wide[...] = ref[...].astype(jnp.float32)
        for g in range(groups):
            own_ref[0, n, g] = wide[pl.ds(g, stripe, stride=groups), :].astype(jnp.bfloat16)


def outgoing_kernel(place_ref, own_ref, up_ref, up2_ref, *out_refs):
    lane = lax.rem(place_ref[0], PLANE)
    for flip, out_ref in zip(FLIPS, out_refs):
        ahead = jnp.bitwise_xor(lane, flip) > lane
        out_ref[0] = up_ref[0]

        @pl.when(ahead)
        def _():
            out_ref[1] = own_ref[0]

        @pl.when(jnp.logical_not(ahead))
        def _():
            out_ref[1] = up2_ref[0]


def sums_kernel(place_ref, up_ref, own_ref, *refs):
    back_refs, (level_ref, far_ref, mine_ref) = refs[:3], refs[3:]
    lane = lax.rem(place_ref[0], PLANE)
    level = up_ref[0].astype(jnp.float32)
    mine = own_ref[0].astype(jnp.float32)
    far = jnp.zeros_like(mine)
    for flip, ref in zip(FLIPS, back_refs):
        ahead = jnp.bitwise_xor(lane, flip) > lane
        level = level + ref[0].astype(jnp.float32)
        got = ref[1].astype(jnp.float32)
        mine = mine + jnp.where(ahead, got, 0.0)
        far = far + jnp.where(ahead, 0.0, got)
    level_ref[0] = level.astype(jnp.bfloat16)
    far_ref[0] = far.astype(jnp.bfloat16)
    mine_ref[0] = mine


def total_kernel(mine_ref, down_ref, down2_ref, k_ref, v_ref, wide):
    groups, stripe = mine_ref.shape[-3:-1]
    for n, ref in enumerate((k_ref, v_ref)):
        for g in range(groups):
            wide[pl.ds(g, stripe, stride=groups), :] = (
                mine_ref[0, n, g] + down_ref[0, n, g].astype(jnp.float32) + down2_ref[0, n, g].astype(jnp.float32)
            )
        ref[...] = wide[...].astype(jnp.bfloat16)


def shards(queries, key_vectors, value_matrix, grad_out, doc_lengths):
    stripe, heads, dim = queries.shape
    groups = key_vectors.shape[1]
    heads_per = heads // groups
    cols = stripe * heads_per
    length = lax.axis_size("ctx")
    me = lax.axis_index("ctx").astype(jnp.int32)
    place = me[None]

    def send(array, to):
        return lax.ppermute(array, "ctx", [(i, to(i)) for i in range(length)])

    def columns(array):
        return array.reshape(stripe, groups, heads_per, dim).transpose(1, 0, 2, 3).reshape(groups, cols, dim)

    def small(body, ins, shapes, scratch=()):
        return pl.pallas_call(
            body,
            out_shape=shapes,
            in_specs=[SMEM if x is place else VMEM for x in ins],
            out_specs=[VMEM] * len(shapes),
            scratch_shapes=list(scratch),
            compiler_params=pltpu.CompilerParams(vmem_limit_bytes=8 << 20),
        )(*ins)

    def shaped(dtype, *dims):
        return jax.ShapeDtypeStruct(dims + (2, groups, stripe, dim), dtype)

    flat = (stripe * groups, dim)
    wide = pltpu.VMEM(flat, jnp.float32)
    (own,) = small(pack_kernel, [key_vectors.reshape(flat), value_matrix.reshape(flat)], [shaped(jnp.bfloat16, 1)], [wide])
    q, do = columns(queries), columns(grad_out)
    stat = jax.ShapeDtypeStruct((groups, 1, cols), jnp.float32)
    total = jax.ShapeDtypeStruct((groups, dim, cols), jnp.float32)
    row = pltpu.VMEM((1, cols), jnp.int32)
    n_docs = doc_lengths.shape[0]
    pair_flops = groups * stripe * cols * dim * 2

    def params(products, n):
        return dict(
            compiler_params=pltpu.CompilerParams(vmem_limit_bytes=8 << 20),
            cost_estimate=pl.CostEstimate(flops=products * n * pair_flops * 2, bytes_accessed=1 << 20, transcendentals=0),
        )

    def stats(slots, kvs, old=None, last=False):
        return pl.pallas_call(
            functools.partial(stats_kernel, slots, heads_per, n_docs, old is None, last),
            out_shape=[stat] * 3,
            in_specs=[SMEM, SMEM] + [VMEM] * (2 + len(kvs) + (0 if old is None else 3)),
            out_specs=[VMEM] * 3,
            scratch_shapes=[row, row],
            input_output_aliases={} if old is None else {4 + len(kvs) + i: i for i in range(3)},
            **params(2, sum(len(held) for held in slots)),
        )(place, doc_lengths, q, do, *kvs, *(old or ()))

    def grads(slots, kvs, m, d, old=None, last=False):
        n = len(kvs)
        dq_shape = [jax.ShapeDtypeStruct(q.shape, jnp.bfloat16), total] if last else [total]
        outs = pl.pallas_call(
            functools.partial(grad_kernel, slots, heads_per, n_docs, old is None, last),
            out_shape=[jax.ShapeDtypeStruct(kv.shape, jnp.bfloat16) for kv in kvs] + dq_shape,
            in_specs=[SMEM, SMEM] + [VMEM] * (4 + n + (0 if old is None else 1)),
            out_specs=[VMEM] * (n + len(dq_shape)),
            scratch_shapes=[row, row],
            input_output_aliases={} if old is None else {6 + n: n + len(dq_shape) - 1},
            **params(5, sum(len(held) for held in slots)),
        )(place, doc_lengths, q, do, m, d, *kvs, *(() if old is None else (old,)))
        return outs[:n], outs[n]

    flip_slots = [[functools.partial(upx_slot, f), functools.partial(mix_slot, f)] for f in FLIPS]

    def shift(array, by):
        return send(array, lambda i: (i + by) % length)

    def swap(array, flip):
        return send(array, lambda i: i ^ flip)

    up2 = shift(own, 2 * PLANE)
    up = shift(own, PLANE)
    seen = stats([[own_slot]], [own])
    up, up2, seen = lax.optimization_barrier((up, up2, seen))
    outgoing = small(outgoing_kernel, [place, own, up, up2], [shaped(jnp.bfloat16, 2)] * 3)
    pairs = [swap(x, f) for x, f in zip(outgoing, FLIPS)]
    seen = stats([[up_slot]], [up], seen)
    for k in (2, 1, 0):
        seen = stats([flip_slots[k]], [pairs[k]], seen, last=k == 0)
    m, _, d = seen

    dq, back = None, [None] * 3
    for k in (2, 1, 0):
        (part,), dq = grads([flip_slots[k]], [pairs[k]], m, d, dq)
        back[k] = swap(part, FLIPS[k])
    (up_part, own_part), dq = grads([[up_slot], [own_slot]], [up, own], m, d, dq, last=True)
    level, far, mine = small(
        sums_kernel,
        [place, up_part, own_part, *back],
        [shaped(jnp.bfloat16, 1), shaped(jnp.bfloat16, 1), shaped(jnp.float32, 1)],
    )
    down2 = shift(far, -2 * PLANE)
    down = shift(level, -PLANE)
    flat_out = jax.ShapeDtypeStruct(flat, jnp.bfloat16)
    grad_k, grad_v = small(total_kernel, [mine, down, down2], [flat_out, flat_out], [wide])
    dq = dq.reshape(groups, stripe, heads_per, dim).transpose(1, 0, 2, 3).reshape(stripe, heads, dim)
    return dq, grad_k.reshape(key_vectors.shape), grad_v.reshape(value_matrix.shape)


def solution(mesh):
    spec = P("ctx", "tp", None)
    return jax.shard_map(
        shards,
        mesh=mesh,
        in_specs=(spec, spec, spec, spec, P()),
        out_specs=(spec, spec, spec),
        check_vma=False,
    )
```

```python
import functools
import math

import jax
import jax.numpy as jnp
from jax import lax
from jax.experimental import pallas as pl
from jax.experimental.pallas import tpu as pltpu
from jax.sharding import PartitionSpec as P


PLANE = 4
FLIPS = (3, 2, 1)
LOG2E = math.log2(math.e)
NEG_INIT = -1e30
NEG_DEAD = -2e30

NT = (((1,), (1,)), ((), ()))
NN = (((1,), (0,)), ((), ()))
TN = (((0,), (0,)), ((), ()))
SMEM = pl.BlockSpec(memory_space=pltpu.SMEM)
VMEM = pl.BlockSpec(memory_space=pltpu.VMEM)


def mm(a, b, dims):
    return lax.dot_general(a, b, dims, preferred_element_type=jnp.float32)


def own_slot(me, lane):
    return me


def up_slot(me, lane):
    return me - PLANE


def upx_slot(flip, me, lane):
    return me - PLANE - lane + jnp.bitwise_xor(lane, flip)


def mix_slot(flip, me, lane):
    other = jnp.bitwise_xor(lane, flip)
    return me - lane + other - jnp.where(other < lane, 0, 2 * PLANE)


def first_live(place_ref):
    me = place_ref[0]
    return me, lax.rem(me, PLANE), place_ref[1]


def start_kernel(heads_per, n_docs, place_ref, lens_ref, start_ref, info_ref):
    groups_cols = start_ref.shape
    stripe = groups_cols[1] // heads_per
    me = place_ref[0]
    col = lax.broadcasted_iota(jnp.int32, groups_cols, 1)
    start = jnp.zeros(groups_cols, jnp.int32)
    end = jnp.int32(0)
    first_key = jnp.int32(0)
    for n in range(n_docs):
        end = end + lens_ref[n]
        start = jnp.where(col >= (end - me * stripe) * heads_per, end, start)
        first_key = jnp.where(me * stripe >= end, end, first_key)
    start_ref[...] = start
    info_ref[0] = me
    info_ref[1] = first_key


def logits(keys, q_g, base, start_ref, heads_per, causal, scale2):
    s = mm(keys, q_g, NT) * scale2
    row = lax.broadcasted_iota(jnp.int32, s.shape, 0)
    live = row >= start_ref[...] - base
    if causal:
        live = live & (row <= lax.div(lax.broadcasted_iota(jnp.int32, start_ref.shape, 1), heads_per))
    return jnp.where(live, s, NEG_DEAD)


def stats_kernel(slots, heads_per, first, last, *refs):
    n = len(slots)
    place_ref, start_ref, q_ref, do_ref = refs[:4]
    kv_refs = refs[4 : 4 + n]
    refs = refs[4 + n :]
    if not first:
        refs = refs[3:]
    m_ref, l_ref, d_ref = refs
    groups, _, dim = q_ref.shape
    stripe = kv_refs[0].shape[-2]
    scale2 = dim**-0.5 * LOG2E
    me, lane, first_key = first_live(place_ref)
    if first:
        m_ref[...] = jnp.full_like(m_ref, NEG_INIT)
        l_ref[...] = jnp.zeros_like(l_ref)
        d_ref[...] = jnp.zeros_like(d_ref)
    for kv_ref, slot in zip(kv_refs, slots):
        at = slot(me, lane)

        @pl.when((at >= 0) & ((at + 1) * stripe > first_key))
        def _():
            for g in range(groups):
                s = logits(kv_ref[0, g], q_ref[g], at * stripe, start_ref, heads_per, slot is own_slot, scale2)
                gp = mm(kv_ref[1, g], do_ref[g], NT)
                m_old = m_ref[g]
                m_new = jnp.maximum(m_old, jnp.max(s, axis=0, keepdims=True))
                e = jnp.exp2(s - m_new)
                fade = jnp.exp2(m_old - m_new)
                m_ref[g] = m_new
                l_ref[g] = l_ref[g] * fade + jnp.sum(e, axis=0, keepdims=True)
                d_ref[g] = d_ref[g] * fade + jnp.sum(e * gp, axis=0, keepdims=True)

    if last:
        d_ref[...] = d_ref[...] / l_ref[...]
        m_ref[...] = m_ref[...] + jnp.log2(l_ref[...])


def grad_kernel(slots, heads_per, first, last, *refs):
    n = len(slots)
    place_ref, start_ref, q_ref, do_ref, m_ref, d_ref = refs[:6]
    kv_refs = refs[6 : 6 + n]
    refs = refs[6 + n :]
    if not first:
        refs = refs[1:]
    part_refs = refs[:n]
    dqt = refs[n + 1] if last else refs[n]
    groups, _, dim = q_ref.shape
    stripe = kv_refs[0].shape[-2]
    scale = dim**-0.5
    scale2 = scale * LOG2E
    me, lane, first_key = first_live(place_ref)
    if first:
        dqt[...] = jnp.zeros_like(dqt)
    for kv_ref, part_ref, slot in zip(kv_refs, part_refs, slots):
        at = slot(me, lane)
        live = (at >= 0) & ((at + 1) * stripe > first_key)

        @pl.when(live)
        def _():
            for g in range(groups):
                keys, vals, q_g, do_g = kv_ref[0, g], kv_ref[1, g], q_ref[g], do_ref[g]
                s = logits(keys, q_g, at * stripe, start_ref, heads_per, slot is own_slot, scale2)
                gp = mm(vals, do_g, NT)
                p = jnp.exp2(s - m_ref[g])
                ds = (p * (gp - d_ref[g])).astype(jnp.bfloat16)
                part_ref[1, g] = mm(p.astype(jnp.bfloat16), do_g, NN).astype(jnp.bfloat16)
                part_ref[0, g] = (mm(ds, q_g, NN) * scale).astype(jnp.bfloat16)
                dqt[g] = dqt[g] + mm(keys, ds, TN)

        @pl.when(jnp.logical_not(live))
        def _():
            part_ref[...] = jnp.zeros_like(part_ref)

    if last:
        for g in range(groups):
            refs[n][g] = (dqt[g] * scale).T.astype(jnp.bfloat16)


def pack_kernel(k_ref, v_ref, own_ref, wide):
    groups, stripe = own_ref.shape[-3:-1]
    for n, ref in enumerate((k_ref, v_ref)):
        wide[...] = ref[...].astype(jnp.float32)
        for g in range(groups):
            own_ref[n, g] = wide[pl.ds(g, stripe, stride=groups), :].astype(jnp.bfloat16)


def outgoing_kernel(place_ref, own_ref, up2_ref, *out_refs):
    lane = lax.rem(place_ref[0], PLANE)
    for flip, out_ref in zip(FLIPS, out_refs):
        ahead = jnp.bitwise_xor(lane, flip) > lane

        @pl.when(ahead)
        def _():
            out_ref[...] = own_ref[...]

        @pl.when(jnp.logical_not(ahead))
        def _():
            out_ref[...] = up2_ref[...]


def far_kernel(place_ref, *refs):
    mix_refs, (far_ref, mine_ref) = refs[:3], refs[3:]
    lane = lax.rem(place_ref[0], PLANE)
    mine = jnp.zeros(mine_ref.shape, jnp.float32)
    far = jnp.zeros_like(mine)
    for flip, ref in zip(FLIPS, mix_refs):
        ahead = jnp.bitwise_xor(lane, flip) > lane
        got = ref[...].astype(jnp.float32)
        mine = mine + jnp.where(ahead, got, 0.0)
        far = far + jnp.where(ahead, 0.0, got)
    far_ref[...] = far.astype(jnp.bfloat16)
    mine_ref[...] = mine


def level_kernel(*refs):
    total = refs[0][...].astype(jnp.float32)
    for ref in refs[1:-1]:
        total = total + ref[...].astype(jnp.float32)
    refs[-1][...] = total.astype(jnp.bfloat16)


def total_kernel(mine_ref, own_ref, down_ref, k_ref, v_ref, wide):
    groups, stripe = mine_ref.shape[-3:-1]
    for n, ref in enumerate((k_ref, v_ref)):
        for g in range(groups):
            wide[pl.ds(g, stripe, stride=groups), :] = (
                mine_ref[n, g] + own_ref[n, g].astype(jnp.float32) + down_ref[n, g].astype(jnp.float32)
            )
        ref[...] = wide[...].astype(jnp.bfloat16)


def shards(queries, key_vectors, value_matrix, grad_out, doc_lengths):
    stripe, heads, dim = queries.shape
    groups = key_vectors.shape[1]
    heads_per = heads // groups
    cols = stripe * heads_per
    length = lax.axis_size("ctx")
    me = lax.axis_index("ctx").astype(jnp.int32)
    place = me[None]

    def send(array, to):
        return lax.ppermute(array, "ctx", [(i, to(i)) for i in range(length)])

    def columns(array):
        return array.reshape(stripe, groups, heads_per, dim).transpose(1, 0, 2, 3).reshape(groups, cols, dim)

    def small(body, ins, shapes, scratch=()):
        return pl.pallas_call(
            body,
            out_shape=shapes,
            in_specs=[SMEM if x is place else VMEM for x in ins],
            out_specs=[VMEM] * len(shapes),
            scratch_shapes=list(scratch),
            compiler_params=pltpu.CompilerParams(vmem_limit_bytes=8 << 20),
        )(*ins)

    def shaped(dtype):
        return jax.ShapeDtypeStruct((2, groups, stripe, dim), dtype)

    flat = (stripe * groups, dim)
    wide = pltpu.VMEM(flat, jnp.float32)
    (own,) = small(pack_kernel, [key_vectors.reshape(flat), value_matrix.reshape(flat)], [shaped(jnp.bfloat16)], [wide])
    q, do = columns(queries), columns(grad_out)
    stat = jax.ShapeDtypeStruct((groups, 1, cols), jnp.float32)
    total = jax.ShapeDtypeStruct((groups, dim, cols), jnp.float32)
    n_docs = doc_lengths.shape[0]
    pair_flops = groups * stripe * cols * dim * 2
    start, info = pl.pallas_call(
        functools.partial(start_kernel, heads_per, n_docs),
        out_shape=[jax.ShapeDtypeStruct((1, cols), jnp.int32), jax.ShapeDtypeStruct((2,), jnp.int32)],
        in_specs=[SMEM, SMEM],
        out_specs=[VMEM, SMEM],
        compiler_params=pltpu.CompilerParams(vmem_limit_bytes=8 << 20),
    )(place, doc_lengths)

    def params(products, n):
        return dict(
            compiler_params=pltpu.CompilerParams(vmem_limit_bytes=16 << 20),
            cost_estimate=pl.CostEstimate(flops=products * n * pair_flops * 2, bytes_accessed=1 << 20, transcendentals=0),
        )

    def stats(slots, kvs, old=None, last=False):
        return pl.pallas_call(
            functools.partial(stats_kernel, slots, heads_per, old is None, last),
            out_shape=[stat] * 3,
            in_specs=[SMEM] + [VMEM] * (3 + len(kvs) + (0 if old is None else 3)),
            out_specs=[VMEM] * 3,
            input_output_aliases={} if old is None else {4 + len(kvs) + i: i for i in range(3)},
            **params(2, len(kvs)),
        )(info, start, q, do, *kvs, *(old or ()))

    def grads(slots, kvs, old=None, last=False):
        n = len(kvs)
        dq_shape = [jax.ShapeDtypeStruct(q.shape, jnp.bfloat16), total] if last else [total]
        outs = pl.pallas_call(
            functools.partial(grad_kernel, slots, heads_per, old is None, last),
            out_shape=[shaped(jnp.bfloat16)] * n + dq_shape,
            in_specs=[SMEM] + [VMEM] * (5 + n + (0 if old is None else 1)),
            out_specs=[VMEM] * (n + len(dq_shape)),
            input_output_aliases={} if old is None else {6 + n: n + len(dq_shape) - 1},
            **params(5, n),
        )(info, start, q, do, m, d, *kvs, *(() if old is None else (old,)))
        return outs[:n], outs[n]

    upx_slots = [functools.partial(upx_slot, f) for f in FLIPS]
    mix_slots = [functools.partial(mix_slot, f) for f in FLIPS]

    def shift(array, by):
        return send(array, lambda i: (i + by) % length)

    def swap(array, flip):
        return send(array, lambda i: i ^ flip)

    up = shift(own, PLANE)
    seen = stats([own_slot], [own])
    up, seen = lax.optimization_barrier((up, seen))
    up2 = shift(up, PLANE)
    upx = [swap(up, f) for f in FLIPS]
    seen = stats([up_slot], [up], seen)
    outgoing = small(outgoing_kernel, [place, own, up2], [shaped(jnp.bfloat16)] * 3)
    mix = [swap(x, f) for x, f in zip(outgoing, FLIPS)]
    seen = stats(upx_slots, upx, seen)
    for k, f in enumerate(FLIPS):
        seen = stats([mix_slots[k]], [mix[k]], seen, last=k == 2)
    m, _, d = seen

    dq, mixed, level = None, [], []
    for k, f in enumerate(FLIPS):
        (part,), dq = grads([mix_slots[k]], [mix[k]], dq)
        mixed.append(swap(part, f))
    for k, f in enumerate(FLIPS):
        (part,), dq = grads([upx_slots[k]], [upx[k]], dq)
        level.append(swap(part, f))
    (own_part, up_part), dq = grads([own_slot, up_slot], [own, up], dq, last=True)

    far, mine = small(far_kernel, [place, *mixed], [shaped(jnp.bfloat16), shaped(jnp.float32)])
    down2 = shift(far, -PLANE)
    (below,) = small(level_kernel, [up_part, down2, *level], [shaped(jnp.bfloat16)])
    down = shift(below, -PLANE)
    flat_out = jax.ShapeDtypeStruct(flat, jnp.bfloat16)
    grad_k, grad_v = small(total_kernel, [mine, own_part, down], [flat_out, flat_out], [wide])
    dq = dq.reshape(groups, stripe, heads_per, dim).transpose(1, 0, 2, 3).reshape(stripe, heads, dim)
    return dq, grad_k.reshape(key_vectors.shape), grad_v.reshape(value_matrix.shape)


def solution(mesh):
    spec = P("ctx", "tp", None)
    return jax.shard_map(
        shards,
        mesh=mesh,
        in_specs=(spec, spec, spec, spec, P()),
        out_specs=(spec, spec, spec),
        check_vma=False,
    )
```

```python
import functools
import math

import jax
import jax.numpy as jnp
from jax import lax
from jax.experimental import pallas as pl
from jax.experimental.pallas import tpu as pltpu
from jax.sharding import PartitionSpec as P


PLANE = 4
FLIPS = (1, 2, 3)
BACK = (2, 1, 0)
LOG2E = math.log2(math.e)
NEG_INIT = -1e30
NEG_DEAD = -2e30

NT = (((1,), (1,)), ((), ()))
NN = (((1,), (0,)), ((), ()))
TN = (((0,), (0,)), ((), ()))
SMEM = pl.BlockSpec(memory_space=pltpu.SMEM)
VMEM = pl.BlockSpec(memory_space=pltpu.VMEM)


def mm(a, b, dims):
    return lax.dot_general(a, b, dims, preferred_element_type=jnp.float32)


def own_slot(me, lane):
    return me


def up_slot(me, lane):
    return me - PLANE


def upx_slot(flip, me, lane):
    return me - PLANE - lane + jnp.bitwise_xor(lane, flip)


def mix_slot(flip, me, lane):
    other = jnp.bitwise_xor(lane, flip)
    return me - lane + other - jnp.where(other < lane, 0, 2 * PLANE)


def first_live(place_ref, start_ref):
    me = place_ref[0]
    return me, lax.rem(me, PLANE), jnp.min(start_ref[:, :128])


def start_kernel(heads_per, n_docs, place_ref, lens_ref, start_ref):
    groups_cols = start_ref.shape
    stripe = groups_cols[1] // heads_per
    me = place_ref[0]
    col = lax.broadcasted_iota(jnp.int32, groups_cols, 1)
    start = jnp.zeros(groups_cols, jnp.int32)
    end = jnp.int32(0)
    for n in range(n_docs):
        end = end + lens_ref[n]
        start = jnp.where(col >= (end - me * stripe) * heads_per, end, start)
    start_ref[...] = start


def logits(keys, q_g, base, start_ref, heads_per, causal, scale2):
    s = mm(keys, q_g, NT) * scale2
    row = lax.broadcasted_iota(jnp.int32, s.shape, 0)
    live = row >= start_ref[...] - base
    if causal:
        live = live & (row <= lax.div(lax.broadcasted_iota(jnp.int32, start_ref.shape, 1), heads_per))
    return jnp.where(live, s, NEG_DEAD)


def stats_kernel(slots, heads_per, first, last, *refs):
    n = len(slots)
    place_ref, start_ref, q_ref, do_ref = refs[:4]
    kv_refs = refs[4 : 4 + n]
    refs = refs[4 + n :]
    if not first:
        refs = refs[3:]
    m_ref, l_ref, d_ref = refs
    groups, _, dim = q_ref.shape
    stripe = kv_refs[0].shape[-2]
    scale2 = dim**-0.5 * LOG2E
    me, lane, first_key = first_live(place_ref, start_ref)
    if first:
        m_ref[...] = jnp.full_like(m_ref, NEG_INIT)
        l_ref[...] = jnp.zeros_like(l_ref)
        d_ref[...] = jnp.zeros_like(d_ref)
    for kv_ref, slot in zip(kv_refs, slots):
        at = slot(me, lane)

        @pl.when((at >= 0) & ((at + 1) * stripe > first_key))
        def _():
            for g in range(groups):
                s = logits(kv_ref[0, g], q_ref[g], at * stripe, start_ref, heads_per, slot is own_slot, scale2)
                gp = mm(kv_ref[1, g], do_ref[g], NT)
                m_old = m_ref[g]
                m_new = jnp.maximum(m_old, jnp.max(s, axis=0, keepdims=True))
                e = jnp.exp2(s - m_new)
                fade = jnp.exp2(m_old - m_new)
                m_ref[g] = m_new
                l_ref[g] = l_ref[g] * fade + jnp.sum(e, axis=0, keepdims=True)
                d_ref[g] = d_ref[g] * fade + jnp.sum(e * gp, axis=0, keepdims=True)

    if last:
        d_ref[...] = d_ref[...] / l_ref[...]
        m_ref[...] = m_ref[...] + jnp.log2(l_ref[...])


def grad_kernel(slots, heads_per, first, last, *refs):
    n = len(slots)
    place_ref, start_ref, q_ref, do_ref, m_ref, d_ref = refs[:6]
    kv_refs = refs[6 : 6 + n]
    refs = refs[6 + n :]
    if not first:
        refs = refs[1:]
    part_refs = refs[:n]
    dqt = refs[n + 1] if last else refs[n]
    groups, _, dim = q_ref.shape
    stripe = kv_refs[0].shape[-2]
    scale = dim**-0.5
    scale2 = scale * LOG2E
    me, lane, first_key = first_live(place_ref, start_ref)
    if first:
        dqt[...] = jnp.zeros_like(dqt)
    for kv_ref, part_ref, slot in zip(kv_refs, part_refs, slots):
        at = slot(me, lane)
        live = (at >= 0) & ((at + 1) * stripe > first_key)

        @pl.when(live)
        def _():
            for g in range(groups):
                keys, vals, q_g, do_g = kv_ref[0, g], kv_ref[1, g], q_ref[g], do_ref[g]
                s = logits(keys, q_g, at * stripe, start_ref, heads_per, slot is own_slot, scale2)
                gp = mm(vals, do_g, NT)
                p = jnp.exp2(s - m_ref[g])
                ds = (p * (gp - d_ref[g])).astype(jnp.bfloat16)
                part_ref[1, g] = mm(p.astype(jnp.bfloat16), do_g, NN).astype(jnp.bfloat16)
                part_ref[0, g] = (mm(ds, q_g, NN) * scale).astype(jnp.bfloat16)
                dqt[g] = dqt[g] + mm(keys, ds, TN)

        @pl.when(jnp.logical_not(live))
        def _():
            part_ref[...] = jnp.zeros_like(part_ref)

    if last:
        for g in range(groups):
            refs[n][g] = (dqt[g] * scale).T.astype(jnp.bfloat16)


def pack_kernel(k_hbm, v_hbm, own_ref, wide, narrow, sems):
    groups, stripe = own_ref.shape[-3:-1]
    copies = [pltpu.make_async_copy(x, narrow.at[n], sems.at[n]) for n, x in enumerate((k_hbm, v_hbm))]
    for copy in copies:
        copy.start()
    for n, copy in enumerate(copies):
        copy.wait()
        wide[...] = narrow[n].astype(jnp.float32)
        for g in range(groups):
            own_ref[n, g] = wide[pl.ds(g, stripe, stride=groups), :].astype(jnp.bfloat16)


def outgoing_kernel(place_ref, own_ref, up2_ref, *out_refs):
    lane = lax.rem(place_ref[0], PLANE)
    for flip, out_ref in zip(FLIPS, out_refs):
        ahead = jnp.bitwise_xor(lane, flip) > lane

        @pl.when(ahead)
        def _():
            out_ref[...] = own_ref[...]

        @pl.when(jnp.logical_not(ahead))
        def _():
            out_ref[...] = up2_ref[...]


def far_kernel(place_ref, *refs):
    mix_refs, (far_ref, mine_ref) = refs[:3], refs[3:]
    lane = lax.rem(place_ref[0], PLANE)
    mine = jnp.zeros(mine_ref.shape, jnp.float32)
    far = jnp.zeros_like(mine)
    for flip, ref in zip(FLIPS, mix_refs):
        ahead = jnp.bitwise_xor(lane, flip) > lane
        got = ref[...].astype(jnp.float32)
        mine = mine + jnp.where(ahead, got, 0.0)
        far = far + jnp.where(ahead, 0.0, got)
    far_ref[...] = far.astype(jnp.bfloat16)
    mine_ref[...] = mine


def level_kernel(*refs):
    total = refs[0][...].astype(jnp.float32)
    for ref in refs[1:-1]:
        total = total + ref[...].astype(jnp.float32)
    refs[-1][...] = total.astype(jnp.bfloat16)


def total_kernel(mine_ref, own_ref, down_ref, k_ref, v_ref, wide):
    groups, stripe = mine_ref.shape[-3:-1]
    for n, ref in enumerate((k_ref, v_ref)):
        for g in range(groups):
            wide[pl.ds(g, stripe, stride=groups), :] = (
                mine_ref[n, g] + own_ref[n, g].astype(jnp.float32) + down_ref[n, g].astype(jnp.float32)
            )
        ref[...] = wide[...].astype(jnp.bfloat16)


def shards(queries, key_vectors, value_matrix, grad_out, doc_lengths):
    stripe, heads, dim = queries.shape
    groups = key_vectors.shape[1]
    heads_per = heads // groups
    cols = stripe * heads_per
    length = lax.axis_size("ctx")
    me = lax.axis_index("ctx").astype(jnp.int32)
    place = me[None]

    def send(array, to):
        return lax.ppermute(array, "ctx", [(i, to(i)) for i in range(length)])

    def columns(array):
        return array.reshape(stripe, groups, heads_per, dim).transpose(1, 0, 2, 3).reshape(groups, cols, dim)

    def small(body, ins, shapes, scratch=(), where=VMEM):
        return pl.pallas_call(
            body,
            out_shape=shapes,
            in_specs=[SMEM if x is place else where for x in ins],
            out_specs=[VMEM] * len(shapes),
            scratch_shapes=list(scratch),
            compiler_params=pltpu.CompilerParams(vmem_limit_bytes=8 << 20),
        )(*ins)

    def shaped(dtype):
        return jax.ShapeDtypeStruct((2, groups, stripe, dim), dtype)

    flat = (stripe * groups, dim)
    wide = pltpu.VMEM(flat, jnp.float32)
    (own,) = small(pack_kernel, [pltpu.with_memory_space_constraint(x.reshape(flat), pltpu.HBM) for x in (key_vectors, value_matrix)], [shaped(jnp.bfloat16)], [wide, pltpu.VMEM((2,) + flat, jnp.bfloat16), pltpu.SemaphoreType.DMA((2,))], pl.BlockSpec(memory_space=pltpu.HBM))
    q, do = columns(queries), columns(grad_out)
    stat = jax.ShapeDtypeStruct((groups, 1, cols), jnp.float32)
    total = jax.ShapeDtypeStruct((groups, dim, cols), jnp.float32)
    n_docs = doc_lengths.shape[0]
    pair_flops = groups * stripe * cols * dim * 2
    (start,) = pl.pallas_call(
        functools.partial(start_kernel, heads_per, n_docs),
        out_shape=[jax.ShapeDtypeStruct((1, cols), jnp.int32)],
        in_specs=[SMEM, SMEM],
        out_specs=[VMEM],
        compiler_params=pltpu.CompilerParams(vmem_limit_bytes=8 << 20),
    )(place, doc_lengths)

    def params(products, n):
        return dict(
            compiler_params=pltpu.CompilerParams(vmem_limit_bytes=16 << 20),
            cost_estimate=pl.CostEstimate(flops=products * n * pair_flops * 2, bytes_accessed=1 << 20, transcendentals=0),
        )

    def stats(slots, kvs, old=None, last=False):
        return pl.pallas_call(
            functools.partial(stats_kernel, slots, heads_per, old is None, last),
            out_shape=[stat] * 3,
            in_specs=[SMEM] + [VMEM] * (3 + len(kvs) + (0 if old is None else 3)),
            out_specs=[VMEM] * 3,
            input_output_aliases={} if old is None else {4 + len(kvs) + i: i for i in range(3)},
            **params(2, len(kvs)),
        )(place, start, q, do, *kvs, *(old or ()))

    def grads(slots, kvs, old=None, last=False):
        n = len(kvs)
        dq_shape = [jax.ShapeDtypeStruct(q.shape, jnp.bfloat16), total] if last else [total]
        outs = pl.pallas_call(
            functools.partial(grad_kernel, slots, heads_per, old is None, last),
            out_shape=[shaped(jnp.bfloat16)] * n + dq_shape,
            in_specs=[SMEM] + [VMEM] * (5 + n + (0 if old is None else 1)),
            out_specs=[VMEM] * (n + len(dq_shape)),
            input_output_aliases={} if old is None else {6 + n: n + len(dq_shape) - 1},
            **params(5, n),
        )(place, start, q, do, m, d, *kvs, *(() if old is None else (old,)))
        return outs[:n], outs[n]

    upx_slots = [functools.partial(upx_slot, f) for f in FLIPS]
    mix_slots = [functools.partial(mix_slot, f) for f in FLIPS]

    def shift(array, by):
        return send(array, lambda i: (i + by) % length)

    def swap(array, flip):
        return send(array, lambda i: i ^ flip)

    up = shift(own, PLANE)
    seen = stats([own_slot], [own])
    up, seen = lax.optimization_barrier((up, seen))
    up2 = shift(up, PLANE)
    upx = [swap(up, f) for f in FLIPS]
    seen = stats([up_slot], [up], seen)
    outgoing = small(outgoing_kernel, [place, own, up2], [shaped(jnp.bfloat16)] * 3)
    mix = [swap(x, f) for x, f in zip(outgoing, FLIPS)]
    for k, f in enumerate(FLIPS):
        seen = stats([upx_slots[k]], [upx[k]], seen)
    for k, f in enumerate(FLIPS):
        seen = stats([mix_slots[k]], [mix[k]], seen, last=k == 2)
    m, _, d = seen

    dq, mixed, level = None, [], []
    for k, f in zip(BACK, FLIPS[::-1]):
        (part,), dq = grads([mix_slots[k]], [mix[k]], dq)
        mixed.append(swap(part, f))
    for k, f in zip(BACK, FLIPS[::-1]):
        (part,), dq = grads([upx_slots[k]], [upx[k]], dq)
        level.append(swap(part, f))
    (own_part, up_part), dq = grads([own_slot, up_slot], [own, up], dq, last=True)

    far, mine = small(far_kernel, [place, *mixed[::-1]], [shaped(jnp.bfloat16), shaped(jnp.float32)])
    down2 = shift(far, -PLANE)
    (below,) = small(level_kernel, [up_part, down2, *level], [shaped(jnp.bfloat16)])
    down = shift(below, -PLANE)
    flat_out = jax.ShapeDtypeStruct(flat, jnp.bfloat16)
    grad_k, grad_v = small(total_kernel, [mine, own_part, down], [flat_out, flat_out], [wide])
    dq = dq.reshape(groups, stripe, heads_per, dim).transpose(1, 0, 2, 3).reshape(stripe, heads, dim)
    return dq, grad_k.reshape(key_vectors.shape), grad_v.reshape(value_matrix.shape)


def solution(mesh):
    spec = P("ctx", "tp", None)
    return jax.shard_map(
        shards,
        mesh=mesh,
        in_specs=(spec, spec, spec, spec, P()),
        out_specs=(spec, spec, spec),
        check_vma=False,
    )
```

```python
import functools
import math

import jax
import jax.numpy as jnp
from jax import lax
from jax.experimental import pallas as pl
from jax.experimental.pallas import tpu as pltpu
from jax.sharding import PartitionSpec as P


PLANE = 4
FLIPS = (1, 2, 3)
BACK = (2, 1, 0)
DIAGONAL = 3
LOG2E = math.log2(math.e)
NEG_INIT = -1e30
NEG_DEAD = -2e30

NT = (((1,), (1,)), ((), ()))
NN = (((1,), (0,)), ((), ()))
TN = (((0,), (0,)), ((), ()))
SMEM = pl.BlockSpec(memory_space=pltpu.SMEM)
VMEM = pl.BlockSpec(memory_space=pltpu.VMEM)


def mm(a, b, dims):
    return lax.dot_general(a, b, dims, preferred_element_type=jnp.float32)


def own_slot(me, lane):
    return me


def up_slot(me, lane):
    return me - PLANE


def upx_slot(flip, me, lane):
    return me - PLANE - lane + jnp.bitwise_xor(lane, flip)


def mix_slot(flip, me, lane):
    other = jnp.bitwise_xor(lane, flip)
    return me - lane + other - jnp.where(other < lane, 0, 2 * PLANE)


def first_live(place_ref, start_ref):
    me = place_ref[0]
    return me, lax.rem(me, PLANE), jnp.min(start_ref[:, :128])


def start_kernel(heads_per, n_docs, place_ref, lens_ref, start_ref):
    groups_cols = start_ref.shape
    stripe = groups_cols[1] // heads_per
    me = place_ref[0]
    col = lax.broadcasted_iota(jnp.int32, groups_cols, 1)
    start = jnp.zeros(groups_cols, jnp.int32)
    end = jnp.int32(0)
    for n in range(n_docs):
        end = end + lens_ref[n]
        start = jnp.where(col >= (end - me * stripe) * heads_per, end, start)
    start_ref[...] = start


def logits(keys, q_g, base, start_ref, heads_per, causal, scale2):
    s = mm(keys, q_g, NT) * scale2
    row = lax.broadcasted_iota(jnp.int32, s.shape, 0)
    live = row >= start_ref[...] - base
    if causal:
        live = live & (row <= lax.div(lax.broadcasted_iota(jnp.int32, start_ref.shape, 1), heads_per))
    return jnp.where(live, s, NEG_DEAD)


def stats_kernel(slots, heads_per, first, last, *refs):
    n = len(slots)
    place_ref, start_ref, q_ref, do_ref = refs[:4]
    kv_refs = refs[4 : 4 + n]
    refs = refs[4 + n :]
    if not first:
        refs = refs[3:]
    m_ref, l_ref, d_ref = refs
    groups, _, dim = q_ref.shape
    stripe = kv_refs[0].shape[-2]
    scale2 = dim**-0.5 * LOG2E
    me, lane, first_key = first_live(place_ref, start_ref)
    if first:
        m_ref[...] = jnp.full_like(m_ref, NEG_INIT)
        l_ref[...] = jnp.zeros_like(l_ref)
        d_ref[...] = jnp.zeros_like(d_ref)
    for kv_ref, slot in zip(kv_refs, slots):
        at = slot(me, lane)

        @pl.when((at >= 0) & ((at + 1) * stripe > first_key))
        def _():
            for g in range(groups):
                s = logits(kv_ref[0, g], q_ref[g], at * stripe, start_ref, heads_per, slot is own_slot, scale2)
                gp = mm(kv_ref[1, g], do_ref[g], NT)
                m_old = m_ref[g]
                m_new = jnp.maximum(m_old, jnp.max(s, axis=0, keepdims=True))
                e = jnp.exp2(s - m_new)
                fade = jnp.exp2(m_old - m_new)
                m_ref[g] = m_new
                l_ref[g] = l_ref[g] * fade + jnp.sum(e, axis=0, keepdims=True)
                d_ref[g] = d_ref[g] * fade + jnp.sum(e * gp, axis=0, keepdims=True)

    if last:
        d_ref[...] = d_ref[...] / l_ref[...]
        m_ref[...] = m_ref[...] + jnp.log2(l_ref[...])


def grad_kernel(slots, heads_per, first, last, *refs):
    n = len(slots)
    place_ref, start_ref, q_ref, do_ref, m_ref, d_ref = refs[:6]
    kv_refs = refs[6 : 6 + n]
    refs = refs[6 + n :]
    if not first:
        refs = refs[1:]
    part_refs = refs[:n]
    dqt = refs[n + 1] if last else refs[n]
    groups, _, dim = q_ref.shape
    stripe = kv_refs[0].shape[-2]
    scale = dim**-0.5
    scale2 = scale * LOG2E
    me, lane, first_key = first_live(place_ref, start_ref)
    if first:
        dqt[...] = jnp.zeros_like(dqt)
    for kv_ref, part_ref, slot in zip(kv_refs, part_refs, slots):
        at = slot(me, lane)
        live = (at >= 0) & ((at + 1) * stripe > first_key)

        @pl.when(live)
        def _():
            for g in range(groups):
                keys, vals, q_g, do_g = kv_ref[0, g], kv_ref[1, g], q_ref[g], do_ref[g]
                s = logits(keys, q_g, at * stripe, start_ref, heads_per, slot is own_slot, scale2)
                gp = mm(vals, do_g, NT)
                p = jnp.exp2(s - m_ref[g])
                ds = (p * (gp - d_ref[g])).astype(jnp.bfloat16)
                part_ref[1, g] = mm(p.astype(jnp.bfloat16), do_g, NN).astype(jnp.bfloat16)
                part_ref[0, g] = (mm(ds, q_g, NN) * scale).astype(jnp.bfloat16)
                dqt[g] = dqt[g] + mm(keys, ds, TN)

        @pl.when(jnp.logical_not(live))
        def _():
            part_ref[...] = jnp.zeros_like(part_ref)

    if last:
        for g in range(groups):
            refs[n][g] = (dqt[g] * scale).T.astype(jnp.bfloat16)


def pack_kernel(k_hbm, v_hbm, own_ref, wide, narrow, sems):
    groups, stripe = own_ref.shape[-3:-1]
    copies = [pltpu.make_async_copy(x, narrow.at[n], sems.at[n]) for n, x in enumerate((k_hbm, v_hbm))]
    for copy in copies:
        copy.start()
    for n, copy in enumerate(copies):
        copy.wait()
        wide[...] = narrow[n].astype(jnp.float32)
        for g in range(groups):
            own_ref[n, g] = wide[pl.ds(g, stripe, stride=groups), :].astype(jnp.bfloat16)


def outgoing_kernel(place_ref, own_ref, up2_ref, *out_refs):
    lane = lax.rem(place_ref[0], PLANE)
    for flip, out_ref in zip(FLIPS, out_refs):
        ahead = jnp.bitwise_xor(lane, flip) > lane

        @pl.when(ahead)
        def _():
            out_ref[...] = own_ref[...]

        @pl.when(jnp.logical_not(ahead))
        def _():
            out_ref[...] = up2_ref[...]


def pick_kernel(place_ref, near_ref, far_ref, out_ref):
    lane = lax.rem(place_ref[0], PLANE)
    ahead = jnp.bitwise_xor(lane, DIAGONAL) > lane

    @pl.when(ahead)
    def _():
        out_ref[...] = far_ref[...]

    @pl.when(jnp.logical_not(ahead))
    def _():
        out_ref[...] = near_ref[...]


def far_kernel(place_ref, *refs):
    mix_refs, (far_ref, mine_ref) = refs[:3], refs[3:]
    lane = lax.rem(place_ref[0], PLANE)
    mine = jnp.zeros(mine_ref.shape, jnp.float32)
    far = jnp.zeros_like(mine)
    for flip, ref in zip(FLIPS, mix_refs):
        ahead = jnp.bitwise_xor(lane, flip) > lane
        got = ref[...].astype(jnp.float32)
        mine = mine + jnp.where(ahead, got, 0.0)
        far = far + jnp.where(ahead, 0.0, got)
    far_ref[...] = far.astype(jnp.bfloat16)
    mine_ref[...] = mine


def level_kernel(*refs):
    total = refs[0][...].astype(jnp.float32)
    for ref in refs[1:-1]:
        total = total + ref[...].astype(jnp.float32)
    refs[-1][...] = total.astype(jnp.bfloat16)


def total_kernel(mine_ref, own_ref, down_ref, k_ref, v_ref, wide):
    groups, stripe = mine_ref.shape[-3:-1]
    for n, ref in enumerate((k_ref, v_ref)):
        for g in range(groups):
            wide[pl.ds(g, stripe, stride=groups), :] = (
                mine_ref[n, g] + own_ref[n, g].astype(jnp.float32) + down_ref[n, g].astype(jnp.float32)
            )
        ref[...] = wide[...].astype(jnp.bfloat16)


def shards(queries, key_vectors, value_matrix, grad_out, doc_lengths):
    stripe, heads, dim = queries.shape
    groups = key_vectors.shape[1]
    heads_per = heads // groups
    cols = stripe * heads_per
    length = lax.axis_size("ctx")
    me = lax.axis_index("ctx").astype(jnp.int32)
    place = me[None]

    def send(array, to):
        return lax.ppermute(array, "ctx", [(i, to(i)) for i in range(length)])

    def columns(array):
        return array.reshape(stripe, groups, heads_per, dim).transpose(1, 0, 2, 3).reshape(groups, cols, dim)

    def small(body, ins, shapes, scratch=(), where=VMEM):
        return pl.pallas_call(
            body,
            out_shape=shapes,
            in_specs=[SMEM if x is place else where for x in ins],
            out_specs=[VMEM] * len(shapes),
            scratch_shapes=list(scratch),
            compiler_params=pltpu.CompilerParams(vmem_limit_bytes=8 << 20),
        )(*ins)

    def shaped(dtype):
        return jax.ShapeDtypeStruct((2, groups, stripe, dim), dtype)

    flat = (stripe * groups, dim)
    wide = pltpu.VMEM(flat, jnp.float32)
    (own,) = small(pack_kernel, [pltpu.with_memory_space_constraint(x.reshape(flat), pltpu.HBM) for x in (key_vectors, value_matrix)], [shaped(jnp.bfloat16)], [wide, pltpu.VMEM((2,) + flat, jnp.bfloat16), pltpu.SemaphoreType.DMA((2,))], pl.BlockSpec(memory_space=pltpu.HBM))
    q, do = columns(queries), columns(grad_out)
    stat = jax.ShapeDtypeStruct((groups, 1, cols), jnp.float32)
    total = jax.ShapeDtypeStruct((groups, dim, cols), jnp.float32)
    n_docs = doc_lengths.shape[0]
    pair_flops = groups * stripe * cols * dim * 2
    (start,) = pl.pallas_call(
        functools.partial(start_kernel, heads_per, n_docs),
        out_shape=[jax.ShapeDtypeStruct((1, cols), jnp.int32)],
        in_specs=[SMEM, SMEM],
        out_specs=[VMEM],
        compiler_params=pltpu.CompilerParams(vmem_limit_bytes=8 << 20),
    )(place, doc_lengths)

    def params(products, n):
        return dict(
            compiler_params=pltpu.CompilerParams(vmem_limit_bytes=16 << 20),
            cost_estimate=pl.CostEstimate(flops=products * n * pair_flops * 2, bytes_accessed=1 << 20, transcendentals=0),
        )

    def stats(slots, kvs, old=None, last=False):
        return pl.pallas_call(
            functools.partial(stats_kernel, slots, heads_per, old is None, last),
            out_shape=[stat] * 3,
            in_specs=[SMEM] + [VMEM] * (3 + len(kvs) + (0 if old is None else 3)),
            out_specs=[VMEM] * 3,
            input_output_aliases={} if old is None else {4 + len(kvs) + i: i for i in range(3)},
            **params(2, len(kvs)),
        )(place, start, q, do, *kvs, *(old or ()))

    def grads(slots, kvs, old=None, last=False):
        n = len(kvs)
        dq_shape = [jax.ShapeDtypeStruct(q.shape, jnp.bfloat16), total] if last else [total]
        outs = pl.pallas_call(
            functools.partial(grad_kernel, slots, heads_per, old is None, last),
            out_shape=[shaped(jnp.bfloat16)] * n + dq_shape,
            in_specs=[SMEM] + [VMEM] * (5 + n + (0 if old is None else 1)),
            out_specs=[VMEM] * (n + len(dq_shape)),
            input_output_aliases={} if old is None else {6 + n: n + len(dq_shape) - 1},
            **params(5, n),
        )(place, start, q, do, m, d, *kvs, *(() if old is None else (old,)))
        return outs[:n], outs[n]

    upx_slots = [functools.partial(upx_slot, f) for f in FLIPS]
    mix_slots = [functools.partial(mix_slot, f) for f in FLIPS]

    def shift(array, by):
        return send(array, lambda i: (i + by) % length)

    def swap(array, flip):
        return send(array, lambda i: i ^ flip)

    up = shift(own, PLANE)
    near = swap(own, DIAGONAL)
    seen = stats([own_slot], [own])
    up, seen = lax.optimization_barrier((up, seen))
    upx = [swap(up, f) for f in FLIPS]
    up2 = shift(up, PLANE)
    up3 = shift(upx[2], PLANE)
    seen = stats([up_slot], [up], seen)
    outgoing = small(outgoing_kernel, [place, own, up2], [shaped(jnp.bfloat16)] * 2)
    mix = [swap(x, f) for x, f in zip(outgoing, FLIPS)]
    for k in (2, 0, 1):
        seen = stats([upx_slots[k]], [upx[k]], seen)
    for k in (0, 1):
        seen = stats([mix_slots[k]], [mix[k]], seen)
    up3, seen = lax.optimization_barrier((up3, seen))
    mix += small(pick_kernel, [place, near, up3], [shaped(jnp.bfloat16)])
    seen = stats([mix_slots[2]], [mix[2]], seen, last=True)
    m, _, d = seen

    dq, mixed, level = None, [], []
    for k, f in zip(BACK, FLIPS[::-1]):
        (part,), dq = grads([mix_slots[k]], [mix[k]], dq)
        mixed.append(swap(part, f))
    for k, f in zip(BACK, FLIPS[::-1]):
        (part,), dq = grads([upx_slots[k]], [upx[k]], dq)
        level.append(swap(part, f))
    (own_part, up_part), dq = grads([own_slot, up_slot], [own, up], dq, last=True)

    far, mine = small(far_kernel, [place, *mixed[::-1]], [shaped(jnp.bfloat16), shaped(jnp.float32)])
    down2 = shift(far, -PLANE)
    (below,) = small(level_kernel, [up_part, down2, *level], [shaped(jnp.bfloat16)])
    down = shift(below, -PLANE)
    flat_out = jax.ShapeDtypeStruct(flat, jnp.bfloat16)
    grad_k, grad_v = small(total_kernel, [mine, own_part, down], [flat_out, flat_out], [wide])
    dq = dq.reshape(groups, stripe, heads_per, dim).transpose(1, 0, 2, 3).reshape(stripe, heads, dim)
    return dq, grad_k.reshape(key_vectors.shape), grad_v.reshape(value_matrix.shape)


def solution(mesh):
    spec = P("ctx", "tp", None)
    return jax.shard_map(
        shards,
        mesh=mesh,
        in_specs=(spec, spec, spec, spec, P()),
        out_specs=(spec, spec, spec),
        check_vma=False,
    )
```

```python
import functools
import math

import jax
import jax.numpy as jnp
from jax import lax
from jax.experimental import pallas as pl
from jax.experimental.pallas import tpu as pltpu
from jax.sharding import PartitionSpec as P


PLANE = 4
FLIPS = (1, 2, 3)
BACK = (2, 1, 0)
DIAGONAL = 3
LOG2E = math.log2(math.e)
NEG_INIT = -1e30
NEG_DEAD = -2e30

NT = (((1,), (1,)), ((), ()))
NN = (((1,), (0,)), ((), ()))
TN = (((0,), (0,)), ((), ()))
SMEM = pl.BlockSpec(memory_space=pltpu.SMEM)
VMEM = pl.BlockSpec(memory_space=pltpu.VMEM)


def mm(a, b, dims):
    return lax.dot_general(a, b, dims, preferred_element_type=jnp.float32)


def own_slot(me, lane):
    return me


def up_slot(me, lane):
    return me - PLANE


def upx_slot(flip, me, lane):
    return me - PLANE - lane + jnp.bitwise_xor(lane, flip)


def mix_slot(flip, me, lane):
    other = jnp.bitwise_xor(lane, flip)
    return me - lane + other - jnp.where(other < lane, 0, 2 * PLANE)


def first_live(place_ref, start_ref):
    me = place_ref[0]
    return me, lax.rem(me, PLANE), jnp.min(start_ref[:, :128])


def start_kernel(heads_per, n_docs, place_ref, lens_ref, start_ref):
    groups_cols = start_ref.shape
    stripe = groups_cols[1] // heads_per
    me = place_ref[0]
    col = lax.broadcasted_iota(jnp.int32, groups_cols, 1)
    start = jnp.zeros(groups_cols, jnp.int32)
    end = jnp.int32(0)
    for n in range(n_docs):
        end = end + lens_ref[n]
        start = jnp.where(col >= (end - me * stripe) * heads_per, end, start)
    start_ref[...] = start


def logits(keys, q_g, base, start_ref, heads_per, causal, scale2):
    s = mm(keys, q_g, NT) * scale2
    row = lax.broadcasted_iota(jnp.int32, s.shape, 0)
    live = row >= start_ref[...] - base
    if causal:
        live = live & (row <= lax.div(lax.broadcasted_iota(jnp.int32, start_ref.shape, 1), heads_per))
    return jnp.where(live, s, NEG_DEAD)


def stats_kernel(slots, heads_per, first, last, *refs):
    n = len(slots)
    place_ref, start_ref, q_ref, do_ref = refs[:4]
    kv_refs = refs[4 : 4 + n]
    refs = refs[4 + n :]
    if not first:
        refs = refs[3:]
    m_ref, l_ref, d_ref = refs[:3]
    e_refs, top_refs = refs[3 : 3 + n], refs[3 + n :]
    groups, _, dim = q_ref.shape
    stripe = kv_refs[0].shape[-2]
    scale2 = dim**-0.5 * LOG2E
    me, lane, first_key = first_live(place_ref, start_ref)
    if first:
        m_ref[...] = jnp.full_like(m_ref, NEG_INIT)
        l_ref[...] = jnp.zeros_like(l_ref)
        d_ref[...] = jnp.zeros_like(d_ref)
    for kv_ref, e_ref, top_ref, slot in zip(kv_refs, e_refs, top_refs, slots):
        at = slot(me, lane)

        @pl.when((at >= 0) & ((at + 1) * stripe > first_key))
        def _():
            for g in range(groups):
                s = logits(kv_ref[0, g], q_ref[g], at * stripe, start_ref, heads_per, slot is own_slot, scale2)
                gp = mm(kv_ref[1, g], do_ref[g], NT)
                m_old = m_ref[g]
                m_new = jnp.maximum(m_old, jnp.max(s, axis=0, keepdims=True))
                e = jnp.exp2(s - m_new)
                e_ref[g] = e.astype(jnp.bfloat16)
                top_ref[g] = m_new
                fade = jnp.exp2(m_old - m_new)
                m_ref[g] = m_new
                l_ref[g] = l_ref[g] * fade + jnp.sum(e, axis=0, keepdims=True)
                d_ref[g] = d_ref[g] * fade + jnp.sum(e * gp, axis=0, keepdims=True)

    if last:
        d_ref[...] = d_ref[...] / l_ref[...]
        m_ref[...] = m_ref[...] + jnp.log2(l_ref[...])


def grad_kernel(slots, first, last, *refs):
    n = len(slots)
    place_ref, start_ref, q_ref, do_ref, m_ref, d_ref = refs[:6]
    kv_refs, e_refs, top_refs = refs[6 : 6 + n], refs[6 + n : 6 + 2 * n], refs[6 + 2 * n : 6 + 3 * n]
    refs = refs[6 + 3 * n :]
    if not first:
        refs = refs[1:]
    part_refs = refs[:n]
    dqt = refs[n + 1] if last else refs[n]
    groups, _, dim = q_ref.shape
    stripe = kv_refs[0].shape[-2]
    scale = dim**-0.5
    me, lane, first_key = first_live(place_ref, start_ref)
    if first:
        dqt[...] = jnp.zeros_like(dqt)
    for kv_ref, part_ref, e_ref, top_ref, slot in zip(kv_refs, part_refs, e_refs, top_refs, slots):
        at = slot(me, lane)
        live = (at >= 0) & ((at + 1) * stripe > first_key)

        @pl.when(live)
        def _():
            for g in range(groups):
                keys, vals, q_g, do_g = kv_ref[0, g], kv_ref[1, g], q_ref[g], do_ref[g]
                gp = mm(vals, do_g, NT)
                p = e_ref[g].astype(jnp.float32) * jnp.exp2(top_ref[g] - m_ref[g])
                ds = (p * (gp - d_ref[g])).astype(jnp.bfloat16)
                part_ref[1, g] = mm(p.astype(jnp.bfloat16), do_g, NN).astype(jnp.bfloat16)
                part_ref[0, g] = (mm(ds, q_g, NN) * scale).astype(jnp.bfloat16)
                dqt[g] = dqt[g] + mm(keys, ds, TN)

        @pl.when(jnp.logical_not(live))
        def _():
            part_ref[...] = jnp.zeros_like(part_ref)

    if last:
        for g in range(groups):
            refs[n][g] = (dqt[g] * scale).T.astype(jnp.bfloat16)


def pack_kernel(k_hbm, v_hbm, own_ref, wide, narrow, sems):
    groups, stripe = own_ref.shape[-3:-1]
    copies = [pltpu.make_async_copy(x, narrow.at[n], sems.at[n]) for n, x in enumerate((k_hbm, v_hbm))]
    for copy in copies:
        copy.start()
    for n, copy in enumerate(copies):
        copy.wait()
        wide[...] = narrow[n].astype(jnp.float32)
        for g in range(groups):
            own_ref[n, g] = wide[pl.ds(g, stripe, stride=groups), :].astype(jnp.bfloat16)


def outgoing_kernel(place_ref, own_ref, up2_ref, *out_refs):
    lane = lax.rem(place_ref[0], PLANE)
    for flip, out_ref in zip(FLIPS, out_refs):
        ahead = jnp.bitwise_xor(lane, flip) > lane

        @pl.when(ahead)
        def _():
            out_ref[...] = own_ref[...]

        @pl.when(jnp.logical_not(ahead))
        def _():
            out_ref[...] = up2_ref[...]


def pick_kernel(place_ref, near_ref, far_ref, out_ref):
    lane = lax.rem(place_ref[0], PLANE)
    ahead = jnp.bitwise_xor(lane, DIAGONAL) > lane

    @pl.when(ahead)
    def _():
        out_ref[...] = far_ref[...]

    @pl.when(jnp.logical_not(ahead))
    def _():
        out_ref[...] = near_ref[...]


def far_kernel(place_ref, *refs):
    mix_refs, (far_ref, mine_ref) = refs[:3], refs[3:]
    lane = lax.rem(place_ref[0], PLANE)
    mine = jnp.zeros(mine_ref.shape, jnp.float32)
    far = jnp.zeros_like(mine)
    for flip, ref in zip(FLIPS, mix_refs):
        ahead = jnp.bitwise_xor(lane, flip) > lane
        got = ref[...].astype(jnp.float32)
        mine = mine + jnp.where(ahead, got, 0.0)
        far = far + jnp.where(ahead, 0.0, got)
    far_ref[...] = far.astype(jnp.bfloat16)
    mine_ref[...] = mine


def level_kernel(*refs):
    total = refs[0][...].astype(jnp.float32)
    for ref in refs[1:-1]:
        total = total + ref[...].astype(jnp.float32)
    refs[-1][...] = total.astype(jnp.bfloat16)


def total_kernel(mine_ref, own_ref, down_ref, k_ref, v_ref, wide):
    groups, stripe = mine_ref.shape[-3:-1]
    for n, ref in enumerate((k_ref, v_ref)):
        for g in range(groups):
            wide[pl.ds(g, stripe, stride=groups), :] = (
                mine_ref[n, g] + own_ref[n, g].astype(jnp.float32) + down_ref[n, g].astype(jnp.float32)
            )
        ref[...] = wide[...].astype(jnp.bfloat16)


def shards(queries, key_vectors, value_matrix, grad_out, doc_lengths):
    stripe, heads, dim = queries.shape
    groups = key_vectors.shape[1]
    heads_per = heads // groups
    cols = stripe * heads_per
    length = lax.axis_size("ctx")
    me = lax.axis_index("ctx").astype(jnp.int32)
    place = me[None]

    def send(array, to):
        return lax.ppermute(array, "ctx", [(i, to(i)) for i in range(length)])

    def columns(array):
        return array.reshape(stripe, groups, heads_per, dim).transpose(1, 0, 2, 3).reshape(groups, cols, dim)

    def small(body, ins, shapes, scratch=(), where=VMEM):
        return pl.pallas_call(
            body,
            out_shape=shapes,
            in_specs=[SMEM if x is place else where for x in ins],
            out_specs=[VMEM] * len(shapes),
            scratch_shapes=list(scratch),
            compiler_params=pltpu.CompilerParams(vmem_limit_bytes=8 << 20),
        )(*ins)

    def shaped(dtype):
        return jax.ShapeDtypeStruct((2, groups, stripe, dim), dtype)

    flat = (stripe * groups, dim)
    wide = pltpu.VMEM(flat, jnp.float32)
    (own,) = small(pack_kernel, [pltpu.with_memory_space_constraint(x.reshape(flat), pltpu.HBM) for x in (key_vectors, value_matrix)], [shaped(jnp.bfloat16)], [wide, pltpu.VMEM((2,) + flat, jnp.bfloat16), pltpu.SemaphoreType.DMA((2,))], pl.BlockSpec(memory_space=pltpu.HBM))
    q, do = columns(queries), columns(grad_out)
    stat = jax.ShapeDtypeStruct((groups, 1, cols), jnp.float32)
    weight = jax.ShapeDtypeStruct((groups, stripe, cols), jnp.bfloat16)
    kept = {}
    total = jax.ShapeDtypeStruct((groups, dim, cols), jnp.float32)
    n_docs = doc_lengths.shape[0]
    pair_flops = groups * stripe * cols * dim * 2
    (start,) = pl.pallas_call(
        functools.partial(start_kernel, heads_per, n_docs),
        out_shape=[jax.ShapeDtypeStruct((1, cols), jnp.int32)],
        in_specs=[SMEM, SMEM],
        out_specs=[VMEM],
        compiler_params=pltpu.CompilerParams(vmem_limit_bytes=8 << 20),
    )(place, doc_lengths)

    def params(products, n):
        return dict(
            compiler_params=pltpu.CompilerParams(vmem_limit_bytes=16 << 20),
            cost_estimate=pl.CostEstimate(flops=products * n * pair_flops * 2, bytes_accessed=1 << 20, transcendentals=0),
        )

    def stats(name, slots, kvs, old=None, last=False):
        outs = pl.pallas_call(
            functools.partial(stats_kernel, slots, heads_per, old is None, last),
            out_shape=[stat] * 3 + [weight] * len(kvs) + [stat] * len(kvs),
            in_specs=[SMEM] + [VMEM] * (3 + len(kvs) + (0 if old is None else 3)),
            out_specs=[VMEM] * (3 + 2 * len(kvs)),
            input_output_aliases={} if old is None else {4 + len(kvs) + i: i for i in range(3)},
            **params(2, len(kvs)),
        )(place, start, q, do, *kvs, *(old or ()))
        kept[name] = outs[3:]
        return outs[:3]

    def grads(name, slots, kvs, old=None, last=False):
        n = len(kvs)
        es = [kept[x][0] for x in name.split()]
        tops = [kept[x][1] for x in name.split()]
        dq_shape = [jax.ShapeDtypeStruct(q.shape, jnp.bfloat16), total] if last else [total]
        outs = pl.pallas_call(
            functools.partial(grad_kernel, slots, old is None, last),
            out_shape=[shaped(jnp.bfloat16)] * n + dq_shape,
            in_specs=[SMEM] + [VMEM] * (5 + 3 * n + (0 if old is None else 1)),
            out_specs=[VMEM] * (n + len(dq_shape)),
            input_output_aliases={} if old is None else {6 + 3 * n: n + len(dq_shape) - 1},
            **params(5, n),
        )(place, start, q, do, m, d, *kvs, *es, *tops, *(() if old is None else (old,)))
        return outs[:n], outs[n]

    upx_slots = [functools.partial(upx_slot, f) for f in FLIPS]
    mix_slots = [functools.partial(mix_slot, f) for f in FLIPS]

    def shift(array, by):
        return send(array, lambda i: (i + by) % length)

    def swap(array, flip):
        return send(array, lambda i: i ^ flip)

    up = shift(own, PLANE)
    near = swap(own, DIAGONAL)
    seen = stats("own", [own_slot], [own])
    up, seen = lax.optimization_barrier((up, seen))
    upx = [swap(up, f) for f in FLIPS]
    up2 = shift(up, PLANE)
    up3 = shift(upx[2], PLANE)
    seen = stats("up", [up_slot], [up], seen)
    outgoing = small(outgoing_kernel, [place, own, up2], [shaped(jnp.bfloat16)] * 2)
    mix = [swap(x, f) for x, f in zip(outgoing, FLIPS)]
    for k in (2, 0, 1):
        seen = stats(f"upx{FLIPS[k]}", [upx_slots[k]], [upx[k]], seen)
    for k in (0, 1):
        seen = stats(f"mix{FLIPS[k]}", [mix_slots[k]], [mix[k]], seen)
    up3, seen = lax.optimization_barrier((up3, seen))
    mix += small(pick_kernel, [place, near, up3], [shaped(jnp.bfloat16)])
    seen = stats("mix3", [mix_slots[2]], [mix[2]], seen, last=True)
    m, _, d = seen

    dq, mixed, level = None, [], []
    for k, f in zip(BACK, FLIPS[::-1]):
        (part,), dq = grads(f"mix{f}", [mix_slots[k]], [mix[k]], dq)
        mixed.append(swap(part, f))
    for k, f in zip(BACK, FLIPS[::-1]):
        (part,), dq = grads(f"upx{f}", [upx_slots[k]], [upx[k]], dq)
        level.append(swap(part, f))
    (own_part, up_part), dq = grads("own up", [own_slot, up_slot], [own, up], dq, last=True)

    far, mine = small(far_kernel, [place, *mixed[::-1]], [shaped(jnp.bfloat16), shaped(jnp.float32)])
    down2 = shift(far, -PLANE)
    (below,) = small(level_kernel, [up_part, down2, *level], [shaped(jnp.bfloat16)])
    down = shift(below, -PLANE)
    flat_out = jax.ShapeDtypeStruct(flat, jnp.bfloat16)
    grad_k, grad_v = small(total_kernel, [mine, own_part, down], [flat_out, flat_out], [wide])
    dq = dq.reshape(groups, stripe, heads_per, dim).transpose(1, 0, 2, 3).reshape(stripe, heads, dim)
    return dq, grad_k.reshape(key_vectors.shape), grad_v.reshape(value_matrix.shape)


def solution(mesh):
    spec = P("ctx", "tp", None)
    return jax.shard_map(
        shards,
        mesh=mesh,
        in_specs=(spec, spec, spec, spec, P()),
        out_specs=(spec, spec, spec),
        check_vma=False,
    )
```

```python
import functools
import math

import jax
import jax.numpy as jnp
from jax import lax
from jax.experimental import pallas as pl
from jax.experimental.pallas import tpu as pltpu
from jax.sharding import PartitionSpec as P


PLANE = 4
FLIPS = (1, 2, 3)
DIAGONAL = 3
LOG2E = math.log2(math.e)
NEG_INIT = -1e30
NEG_DEAD = -2e30

NT = (((1,), (1,)), ((), ()))
NN = (((1,), (0,)), ((), ()))
TN = (((0,), (0,)), ((), ()))
SMEM = pl.BlockSpec(memory_space=pltpu.SMEM)
VMEM = pl.BlockSpec(memory_space=pltpu.VMEM)


def mm(a, b, dims):
    return lax.dot_general(a, b, dims, preferred_element_type=jnp.float32)


def own_slot(me, lane):
    return me


def up_slot(me, lane):
    return me - PLANE


def upx_slot(flip, me, lane):
    return me - PLANE - lane + jnp.bitwise_xor(lane, flip)


def mix_slot(flip, me, lane):
    other = jnp.bitwise_xor(lane, flip)
    return me - lane + other - jnp.where(other < lane, 0, 2 * PLANE)


def first_live(place_ref, start_ref):
    me = place_ref[0]
    return me, lax.rem(me, PLANE), jnp.min(start_ref[:, :128])


def start_kernel(heads_per, n_docs, place_ref, lens_ref, start_ref):
    groups_cols = start_ref.shape
    stripe = groups_cols[1] // heads_per
    me = place_ref[0]
    col = lax.broadcasted_iota(jnp.int32, groups_cols, 1)
    start = jnp.zeros(groups_cols, jnp.int32)
    end = jnp.int32(0)
    for n in range(n_docs):
        end = end + lens_ref[n]
        start = jnp.where(col >= (end - me * stripe) * heads_per, end, start)
    start_ref[...] = start


def logits(keys, q_g, base, start_ref, heads_per, causal, scale2):
    s = mm(keys, q_g, NT) * scale2
    row = lax.broadcasted_iota(jnp.int32, s.shape, 0)
    live = row >= start_ref[...] - base
    if causal:
        live = live & (row <= lax.div(lax.broadcasted_iota(jnp.int32, start_ref.shape, 1), heads_per))
    return jnp.where(live, s, NEG_DEAD)


def stats_kernel(slots, heads_per, first, last, *refs):
    n = len(slots)
    place_ref, start_ref, q_ref, do_ref = refs[:4]
    kv_refs = refs[4 : 4 + n]
    refs = refs[4 + n :]
    if not first:
        refs = refs[3:]
    m_ref, l_ref, d_ref = refs[:3]
    e_refs, top_refs = refs[3 : 3 + n], refs[3 + n :]
    groups, _, dim = q_ref.shape
    stripe = kv_refs[0].shape[-2]
    scale2 = dim**-0.5 * LOG2E
    me, lane, first_key = first_live(place_ref, start_ref)
    if first:
        m_ref[...] = jnp.full_like(m_ref, NEG_INIT)
        l_ref[...] = jnp.zeros_like(l_ref)
        d_ref[...] = jnp.zeros_like(d_ref)
    for kv_ref, e_ref, top_ref, slot in zip(kv_refs, e_refs, top_refs, slots):
        at = slot(me, lane)

        @pl.when((at >= 0) & ((at + 1) * stripe > first_key))
        def _():
            for g in range(groups):
                s = logits(kv_ref[0, g], q_ref[g], at * stripe, start_ref, heads_per, slot is own_slot, scale2)
                gp = mm(kv_ref[1, g], do_ref[g], NT)
                m_old = m_ref[g]
                m_new = jnp.maximum(m_old, jnp.max(s, axis=0, keepdims=True))
                e = jnp.exp2(s - m_new)
                e_ref[g] = e.astype(jnp.bfloat16)
                top_ref[g] = m_new
                fade = jnp.exp2(m_old - m_new)
                m_ref[g] = m_new
                l_ref[g] = l_ref[g] * fade + jnp.sum(e, axis=0, keepdims=True)
                d_ref[g] = d_ref[g] * fade + jnp.sum(e * gp, axis=0, keepdims=True)

    if last:
        d_ref[...] = d_ref[...] / l_ref[...]
        m_ref[...] = m_ref[...] + jnp.log2(l_ref[...])


def grad_kernel(slots, first, last, *refs):
    n = len(slots)
    place_ref, start_ref, q_ref, do_ref, m_ref, d_ref = refs[:6]
    kv_refs, e_refs, top_refs = refs[6 : 6 + n], refs[6 + n : 6 + 2 * n], refs[6 + 2 * n : 6 + 3 * n]
    refs = refs[6 + 3 * n :]
    if not first:
        refs = refs[1:]
    part_refs = refs[:n]
    dqt = refs[n + 1] if last else refs[n]
    groups, _, dim = q_ref.shape
    stripe = kv_refs[0].shape[-2]
    scale = dim**-0.5
    me, lane, first_key = first_live(place_ref, start_ref)
    if first:
        dqt[...] = jnp.zeros_like(dqt)
    for kv_ref, part_ref, e_ref, top_ref, slot in zip(kv_refs, part_refs, e_refs, top_refs, slots):
        at = slot(me, lane)
        live = (at >= 0) & ((at + 1) * stripe > first_key)

        @pl.when(live)
        def _():
            for g in range(groups):
                keys, vals, q_g, do_g = kv_ref[0, g], kv_ref[1, g], q_ref[g], do_ref[g]
                gp = mm(vals, do_g, NT)
                p = e_ref[g].astype(jnp.float32) * jnp.exp2(top_ref[g] - m_ref[g])
                ds = (p * (gp - d_ref[g])).astype(jnp.bfloat16)
                part_ref[1, g] = mm(p.astype(jnp.bfloat16), do_g, NN).astype(jnp.bfloat16)
                part_ref[0, g] = (mm(ds, q_g, NN) * scale).astype(jnp.bfloat16)
                dqt[g] = dqt[g] + mm(keys, ds, TN)

        @pl.when(jnp.logical_not(live))
        def _():
            part_ref[...] = jnp.zeros_like(part_ref)

    if last:
        for g in range(groups):
            refs[n][g] = (dqt[g] * scale).T.astype(jnp.bfloat16)


def pack_kernel(k_hbm, v_hbm, own_ref, wide, narrow, sems):
    groups, stripe = own_ref.shape[-3:-1]
    copies = [pltpu.make_async_copy(x, narrow.at[n], sems.at[n]) for n, x in enumerate((k_hbm, v_hbm))]
    for copy in copies:
        copy.start()
    for n, copy in enumerate(copies):
        copy.wait()
        wide[...] = narrow[n].astype(jnp.float32)
        for g in range(groups):
            own_ref[n, g] = wide[pl.ds(g, stripe, stride=groups), :].astype(jnp.bfloat16)


def outgoing_kernel(place_ref, own_ref, up2_ref, *out_refs):
    lane = lax.rem(place_ref[0], PLANE)
    for flip, out_ref in zip(FLIPS, out_refs):
        ahead = jnp.bitwise_xor(lane, flip) > lane

        @pl.when(ahead)
        def _():
            out_ref[...] = own_ref[...]

        @pl.when(jnp.logical_not(ahead))
        def _():
            out_ref[...] = up2_ref[...]


def pick_kernel(place_ref, near_ref, far_ref, out_ref):
    lane = lax.rem(place_ref[0], PLANE)
    ahead = jnp.bitwise_xor(lane, DIAGONAL) > lane

    @pl.when(ahead)
    def _():
        out_ref[...] = far_ref[...]

    @pl.when(jnp.logical_not(ahead))
    def _():
        out_ref[...] = near_ref[...]


def join_kernel(place_ref, part_ref, above_ref, out_ref):
    lane = lax.rem(place_ref[0], PLANE)
    ahead = jnp.bitwise_xor(lane, DIAGONAL) > lane
    above = jnp.where(ahead, above_ref[...].astype(jnp.float32), 0.0)
    out_ref[...] = (part_ref[...].astype(jnp.float32) + above).astype(jnp.bfloat16)


def far_kernel(place_ref, *refs):
    mix_refs, (far_ref, mine_ref) = refs[:2], refs[2:]
    lane = lax.rem(place_ref[0], PLANE)
    mine = jnp.zeros(mine_ref.shape, jnp.float32)
    far = jnp.zeros_like(mine)
    for flip, ref in zip(FLIPS, mix_refs):
        ahead = jnp.bitwise_xor(lane, flip) > lane
        got = ref[...].astype(jnp.float32)
        mine = mine + jnp.where(ahead, got, 0.0)
        far = far + jnp.where(ahead, 0.0, got)
    far_ref[...] = far.astype(jnp.bfloat16)
    mine_ref[...] = mine


def level_kernel(*refs):
    total = refs[0][...].astype(jnp.float32)
    for ref in refs[1:-1]:
        total = total + ref[...].astype(jnp.float32)
    refs[-1][...] = total.astype(jnp.bfloat16)


def total_kernel(place_ref, mine_ref, own_ref, down_ref, near_ref, k_ref, v_ref, wide):
    lane = lax.rem(place_ref[0], PLANE)
    ahead = jnp.bitwise_xor(lane, DIAGONAL) > lane
    groups, stripe = mine_ref.shape[-3:-1]
    for n, ref in enumerate((k_ref, v_ref)):
        for g in range(groups):
            near = jnp.where(ahead, near_ref[n, g].astype(jnp.float32), 0.0)
            wide[pl.ds(g, stripe, stride=groups), :] = (
                mine_ref[n, g] + own_ref[n, g].astype(jnp.float32) + down_ref[n, g].astype(jnp.float32) + near
            )
        ref[...] = wide[...].astype(jnp.bfloat16)


def shards(queries, key_vectors, value_matrix, grad_out, doc_lengths):
    stripe, heads, dim = queries.shape
    groups = key_vectors.shape[1]
    heads_per = heads // groups
    cols = stripe * heads_per
    length = lax.axis_size("ctx")
    me = lax.axis_index("ctx").astype(jnp.int32)
    place = me[None]

    def send(array, to):
        return lax.ppermute(array, "ctx", [(i, to(i)) for i in range(length)])

    def columns(array):
        return array.reshape(stripe, groups, heads_per, dim).transpose(1, 0, 2, 3).reshape(groups, cols, dim)

    def small(body, ins, shapes, scratch=(), where=VMEM):
        return pl.pallas_call(
            body,
            out_shape=shapes,
            in_specs=[SMEM if x is place else where for x in ins],
            out_specs=[VMEM] * len(shapes),
            scratch_shapes=list(scratch),
            compiler_params=pltpu.CompilerParams(vmem_limit_bytes=8 << 20),
        )(*ins)

    def shaped(dtype):
        return jax.ShapeDtypeStruct((2, groups, stripe, dim), dtype)

    flat = (stripe * groups, dim)
    wide = pltpu.VMEM(flat, jnp.float32)
    (own,) = small(pack_kernel, [pltpu.with_memory_space_constraint(x.reshape(flat), pltpu.HBM) for x in (key_vectors, value_matrix)], [shaped(jnp.bfloat16)], [wide, pltpu.VMEM((2,) + flat, jnp.bfloat16), pltpu.SemaphoreType.DMA((2,))], pl.BlockSpec(memory_space=pltpu.HBM))
    q, do = columns(queries), columns(grad_out)
    stat = jax.ShapeDtypeStruct((groups, 1, cols), jnp.float32)
    weight = jax.ShapeDtypeStruct((groups, stripe, cols), jnp.bfloat16)
    kept = {}
    total = jax.ShapeDtypeStruct((groups, dim, cols), jnp.float32)
    n_docs = doc_lengths.shape[0]
    pair_flops = groups * stripe * cols * dim * 2
    (start,) = pl.pallas_call(
        functools.partial(start_kernel, heads_per, n_docs),
        out_shape=[jax.ShapeDtypeStruct((1, cols), jnp.int32)],
        in_specs=[SMEM, SMEM],
        out_specs=[VMEM],
        compiler_params=pltpu.CompilerParams(vmem_limit_bytes=8 << 20),
    )(place, doc_lengths)

    def params(products, n):
        return dict(
            compiler_params=pltpu.CompilerParams(vmem_limit_bytes=16 << 20),
            cost_estimate=pl.CostEstimate(flops=products * n * pair_flops * 2, bytes_accessed=1 << 20, transcendentals=0),
        )

    def stats(name, slots, kvs, old=None, last=False):
        outs = pl.pallas_call(
            functools.partial(stats_kernel, slots, heads_per, old is None, last),
            out_shape=[stat] * 3 + [weight] * len(kvs) + [stat] * len(kvs),
            in_specs=[SMEM] + [VMEM] * (3 + len(kvs) + (0 if old is None else 3)),
            out_specs=[VMEM] * (3 + 2 * len(kvs)),
            input_output_aliases={} if old is None else {4 + len(kvs) + i: i for i in range(3)},
            **params(2, len(kvs)),
        )(place, start, q, do, *kvs, *(old or ()))
        for k in range(len(kvs)):
            kept[f"{name}{k + 1}" if len(kvs) > 1 else name] = outs[3 + k], outs[3 + len(kvs) + k]
        return outs[:3]

    def grads(name, slots, kvs, old=None, last=False):
        n = len(kvs)
        es = [kept[x][0] for x in name.split()]
        tops = [kept[x][1] for x in name.split()]
        dq_shape = [jax.ShapeDtypeStruct(q.shape, jnp.bfloat16), total] if last else [total]
        outs = pl.pallas_call(
            functools.partial(grad_kernel, slots, old is None, last),
            out_shape=[shaped(jnp.bfloat16)] * n + dq_shape,
            in_specs=[SMEM] + [VMEM] * (5 + 3 * n + (0 if old is None else 1)),
            out_specs=[VMEM] * (n + len(dq_shape)),
            input_output_aliases={} if old is None else {6 + 3 * n: n + len(dq_shape) - 1},
            **params(5, n),
        )(place, start, q, do, m, d, *kvs, *es, *tops, *(() if old is None else (old,)))
        return outs[:n], outs[n]

    upx_slots = [functools.partial(upx_slot, f) for f in FLIPS]
    mix_slots = [functools.partial(mix_slot, f) for f in FLIPS]

    def shift(array, by):
        return send(array, lambda i: (i + by) % length)

    def swap(array, flip):
        return send(array, lambda i: i ^ flip)

    up = shift(own, PLANE)
    near = swap(own, DIAGONAL)
    seen = stats("own", [own_slot], [own])
    up, seen = lax.optimization_barrier((up, seen))
    upx = [swap(up, f) for f in FLIPS]
    up2 = shift(up, PLANE)
    up3 = shift(upx[2], PLANE)
    seen = stats("up", [up_slot], [up], seen)
    outgoing = small(outgoing_kernel, [place, own, up2], [shaped(jnp.bfloat16)] * 2)
    mix = [swap(x, f) for x, f in zip(outgoing, FLIPS)]
    seen = stats("upx3", upx_slots[2:], upx[2:], seen)
    seen = stats("upx", upx_slots[:2], upx[:2], seen)
    for k in (0, 1):
        seen = stats(f"mix{FLIPS[k]}", [mix_slots[k]], [mix[k]], seen)
    up3, seen = lax.optimization_barrier((up3, seen))
    mix += small(pick_kernel, [place, near, up3], [shaped(jnp.bfloat16)])
    seen = stats("mix3", [mix_slots[2]], [mix[2]], seen, last=True)
    m, _, d = seen

    mixed, level = {}, []
    (diagonal,), dq = grads("mix3", [mix_slots[2]], [mix[2]])
    above = shift(diagonal, -PLANE)
    for k in (1, 0):
        (part,), dq = grads(f"mix{FLIPS[k]}", [mix_slots[k]], [mix[k]], dq)
        mixed[k] = swap(part, FLIPS[k])
    for k in (1, 2, 0):
        (part,), dq = grads(f"upx{FLIPS[k]}", [upx_slots[k]], [upx[k]], dq)
        if FLIPS[k] == DIAGONAL:
            (part,) = small(join_kernel, [place, part, above], [shaped(jnp.bfloat16)])
        level.append(swap(part, FLIPS[k]))
    (own_part, up_part), dq = grads("own up", [own_slot, up_slot], [own, up], dq, last=True)
    near_back = swap(diagonal, DIAGONAL)

    far, mine = small(far_kernel, [place, mixed[0], mixed[1]], [shaped(jnp.bfloat16), shaped(jnp.float32)])
    down2 = shift(far, -PLANE)
    (below,) = small(level_kernel, [up_part, down2, *level], [shaped(jnp.bfloat16)])
    down = shift(below, -PLANE)
    flat_out = jax.ShapeDtypeStruct(flat, jnp.bfloat16)
    grad_k, grad_v = small(total_kernel, [place, mine, own_part, down, near_back], [flat_out, flat_out], [wide])
    dq = dq.reshape(groups, stripe, heads_per, dim).transpose(1, 0, 2, 3).reshape(stripe, heads, dim)
    return dq, grad_k.reshape(key_vectors.shape), grad_v.reshape(value_matrix.shape)


def solution(mesh):
    spec = P("ctx", "tp", None)
    return jax.shard_map(
        shards,
        mesh=mesh,
        in_specs=(spec, spec, spec, spec, P()),
        out_specs=(spec, spec, spec),
        check_vma=False,
    )
```
